32 devices in a mesh: layer: 4 (over z), tile: 8 (over y, x, core).
Axes of the slice: x: 2, y: 2, z: 4, core: 2. Of those that a mesh axis runs over, the one named last changes fastest.
Arguments:
- measured_slopes: float32 [6, 2, 96, 4096], P(None, None, 'tile'), may hold values from -18 to 18
- valid_mask: int32 [96, 4096], P('tile'), may hold values 0 or 1
- layer_offsets: int32 [6, 4, 2], replicated, may hold values from -8 to 8, as said below
- reg_weight: float32 [4], replicated, may hold values from 0.01 to 0.1
Outputs:
- layer_estimate: float32 [4, 96, 4096], P('layer', 'tile')
- residual: float32 [4, 96, 4096], P('layer', 'tile')
The draws below stay inside these ranges and needn't reach their ends.
Inputs may be any that keep to these rules, and one draw needn't show every extreme that they name: `layer_offsets`: every entry lies between -8 and 8; some entry equals 8 and some equals -8.
All inputs are finite; a program needn't handle non-finite values. No bound on the sum of `valid_mask` on one device may be relied on, other than what follows from the above.
Results may differ from the reference program's by a relative error of at most 0.0001.
Values sent between devices are 32-bit elements; how exact they have to be, the bound alone decides.
No kernel may reach another device: no remote copies, remote signals or barrier semaphores. Data moves between devices by JAX's collectives and lax.ppermute only.
A program may use at most 64 MiB of HBM per device.

```python
import math
import jax
import jax.numpy as jnp
from jax import lax

COLS = 4096
DIRS = 6
HALO = 8
ITERS = 2
LAYERS = 4
NR = 96


def draw_measured_slopes(key, part):
    ramp = jnp.arange(NR, dtype=jnp.float32) / (NR - 1)
    base = jnp.clip(jax.random.normal(key, (DIRS, 2, NR, COLS), jnp.float32), -6.0, 6.0)
    scale = 1.0 + 2.0 * ramp
    return (base * scale[:, None]).astype(jnp.float32)


def draw_layer_offsets(key, part):
    drawn = jax.random.randint(key, (DIRS, LAYERS, 2), -HALO, HALO + 1)
    drawn = drawn.at[0, LAYERS - 1, :].set(HALO)
    drawn = drawn.at[1, LAYERS - 1, :].set(-HALO)
    return drawn.astype(jnp.int32)


def plant(values, own_key, low, high):
    dims = values.shape
    index_at = [jax.random.randint(jax.random.fold_in(own_key, axis), (), 0, dims[axis]) for axis in range(len(dims))]
    values = values.at[tuple(index_at)].set(low)
    longest = dims.index(max(dims))
    index_at[longest] = (index_at[longest] + 1) % dims[longest]
    return values.at[tuple(index_at)].set(high)


def setup_inputs(seed: int = 0) -> dict:
    arg_keys = jax.random.split(jax.random.key(seed), 5)
    return {
        "measured_slopes": draw_measured_slopes(jax.random.fold_in(arg_keys[4], 71), 0),
        "valid_mask": plant((jax.random.randint(arg_keys[1], (NR, COLS), 0, 8) < 7).astype(jnp.int32), jax.random.fold_in(arg_keys[1], 1), 0, 1),
        "layer_offsets": draw_layer_offsets(jax.random.fold_in(arg_keys[4], 71), 0),
        "reg_weight": jnp.clip(jnp.exp(jax.random.uniform(arg_keys[3], (LAYERS,), jnp.float32, math.log(0.01), math.log(0.1))), 0.01, 0.1),
    }


def shift_field(field, row_shift, col_shift):
    padded = jnp.pad(field, ((HALO, HALO), (HALO, HALO)))
    return lax.dynamic_slice(padded, (HALO + row_shift, HALO + col_shift), field.shape)


def fried_slopes(phase, maskf):
    padded = jnp.pad(phase, ((0, 1), (0, 1)))
    p00 = padded[:-1, :-1]
    p01 = padded[:-1, 1:]
    p10 = padded[1:, :-1]
    p11 = padded[1:, 1:]
    grad_x = 0.5 * (p01 - p00 + p11 - p10)
    grad_y = 0.5 * (p10 - p00 + p11 - p01)
    return maskf * grad_x, maskf * grad_y


def fried_adjoint(slope_x, slope_y):
    summed_x = slope_x + jnp.pad(slope_x, ((1, 0), (0, 0)))[:-1]
    summed_y = slope_y + jnp.pad(slope_y, ((0, 0), (1, 0)))[:, :-1]
    left_x = jnp.pad(summed_x, ((0, 0), (1, 0)))[:, :-1]
    upper_y = jnp.pad(summed_y, ((1, 0), (0, 0)))[:-1]
    return 0.5 * (left_x - summed_x + upper_y - summed_y)


def laplace(field):
    padded = jnp.pad(field, 1)
    return 4.0 * field - padded[:-2, 1:-1] - padded[2:, 1:-1] - padded[1:-1, :-2] - padded[1:-1, 2:]


def back_project(adjoints, layer_offsets, layer):
    total = jnp.zeros(adjoints[0].shape, jnp.float32)
    for direc in range(DIRS):
        total = total + shift_field(adjoints[direc], -layer_offsets[direc, layer, 0], -layer_offsets[direc, layer, 1])
    return total


def reference(measured_slopes, valid_mask, layer_offsets, reg_weight):
    maskf = valid_mask.astype(jnp.float32)

    def apply_operator(stack):
        adjoints = []
        for direc in range(DIRS):
            phase = jnp.zeros(stack.shape[1:], jnp.float32)
            for layer in range(LAYERS):
                phase = phase + shift_field(stack[layer], layer_offsets[direc, layer, 0], layer_offsets[direc, layer, 1])
            slope_x, slope_y = fried_slopes(phase, maskf)
            adjoints.append(fried_adjoint(slope_x, slope_y))
        result = []
        for layer in range(LAYERS):
            total = back_project(adjoints, layer_offsets, layer)
            result.append(total + reg_weight[layer] * laplace(laplace(stack[layer])))
        return jnp.stack(result)

    adjoints = [fried_adjoint(maskf * measured_slopes[direc, 0], maskf * measured_slopes[direc, 1]) for direc in range(DIRS)]
    right_side = jnp.stack([back_project(adjoints, layer_offsets, layer) for layer in range(LAYERS)])
    estimate = jnp.zeros_like(right_side)
    residual = right_side
    direction = right_side
    norm_now = jnp.sum(residual * residual)
    for step in range(ITERS):
        image = apply_operator(direction)
        alpha = norm_now / jnp.sum(direction * image)
        estimate = estimate + alpha * direction
        residual = residual - alpha * image
        norm_next = jnp.sum(residual * residual)
        direction = residual + (norm_next / norm_now) * direction
        norm_now = norm_next
    return estimate, residual
```

```python
import functools

import jax
import jax.numpy as jnp
from jax import lax
from jax.experimental import pallas as pl
from jax.experimental.pallas import tpu as pltpu
from jax.sharding import PartitionSpec as P

HALO = 8
LANES = 128
PAD = 8
REACH_ROW = 2 * (2 * HALO + 1)
REACH = REACH_ROW + HALO + 1
VMEM = pltpu.MemorySpace.VMEM
SMEM = pltpu.MemorySpace.SMEM


def round_up(value, unit):
    return -(-value // unit) * unit


class Plan:
    def __init__(self, mesh, dirs, rows, width, layers):
        self.layer_devices = mesh.shape["layer"]
        self.tiles = mesh.shape["tile"]
        self.devices = self.layer_devices * self.tiles
        self.dirs = dirs
        self.rows = rows
        self.width = width
        self.layers = layers
        self.own_layers = layers // self.layer_devices
        self.grid_rows = rows * self.tiles
        assert width % self.devices == 0 and layers % self.layer_devices == 0
        self.own = width // self.devices
        self.part = width // self.layer_devices
        assert self.part % LANES == 0
        self.lane_tiles = round_up(self.own + 2 * REACH, LANES) // LANES
        self.side = (self.lane_tiles * LANES - self.own) // 2
        self.margin = round_up(self.side + 1, LANES)
        self.strip = self.part + 2 * self.margin
        self.in_rows = round_up(dirs * (rows + 1) + rows, 8)
        self.out_rows = round_up(3 * self.own_layers * rows + 1, 8)


def lane_index():
    return lax.broadcasted_iota(jnp.int32, (8, LANES), 1)


def tall(mask, rows):
    return jnp.broadcast_to(mask[:1], (rows, LANES))


def lane_shift(tiles, steps, rows):
    count = len(tiles)
    if isinstance(steps, int):
        turn = (-steps) % LANES
    else:
        turn = jnp.where(steps > 0, LANES - steps, -steps)
    turned = [pltpu.roll(tile, turn, 1) for tile in tiles]
    if count == 1:
        return turned
    source = lane_index() + steps
    past = tall(source >= LANES, rows)
    before = tall(source < 0, rows)
    if count == 2:
        outside = past | before
        return [jnp.where(outside, turned[1 - t], turned[t]) for t in range(2)]
    return [
        jnp.where(
            past,
            turned[(t + 1) % count],
            jnp.where(before, turned[(t - 1) % count], turned[t]),
        )
        for t in range(count)
    ]


def gather_kernel(plan, place, slopes, mask, out, raw, raw_mask, tall_a, tall_b, strip, sems):
    layer = place[0]
    margin, part = plan.margin, plan.part
    rows, dirs = plan.rows, plan.dirs
    last = plan.layer_devices - 1
    start = pl.multiple_of(layer * part, LANES)

    def copies(source, size, target):
        return (
            pltpu.make_async_copy(
                slopes.at[:, :, :, pl.ds(source, size)],
                raw.at[:, :, :, pl.ds(target, size)],
                sems.at[0],
            ),
            pltpu.make_async_copy(
                mask.at[:, pl.ds(source, size)], raw_mask.at[:, pl.ds(target, size)], sems.at[1]
            ),
        )

    def blank(target):
        raw[:, :, :, target : target + margin] = jnp.zeros((dirs, 2, rows, margin), jnp.float32)
        raw_mask[:, target : target + margin] = jnp.zeros((rows, margin), jnp.int32)

    middle = copies(start, part, margin)
    for copy in middle:
        copy.start()
    for copy in middle:
        copy.wait()

    @pl.when(layer > 0)
    def _():
        left = copies(pl.multiple_of(start - margin, LANES), margin, 0)
        for copy in left:
            copy.start()
        for copy in left:
            copy.wait()

    @pl.when(layer == 0)
    def _():
        blank(0)

    @pl.when(layer < last)
    def _():
        right = copies(pl.multiple_of(start + part, LANES), margin, margin + part)
        for copy in right:
            copy.start()
        for copy in right:
            copy.wait()

    @pl.when(layer == last)
    def _():
        blank(margin + part)

    keep = raw_mask[...].astype(jnp.float32)
    zero_tail = jnp.zeros((16 * (-(-(rows + 1) // 16)) - rows, plan.strip), jnp.float32)
    tall_a[rows:, :] = zero_tail
    tall_b[rows:, :] = zero_tail
    column = lax.broadcasted_iota(jnp.int32, (1, plan.strip), 1) + (start - margin)
    in_grid = jnp.where((column >= 0) & (column < plan.width), 1.0, 0.0)
    strips = plan.strip // LANES
    for n in range(strips):
        lanes = slice(n * LANES, (n + 1) * LANES)
        strip[n, dirs * rows : (dirs + 1) * rows, :] = keep[:, lanes]
        used = dirs * (rows + 1) + rows
        if used < plan.in_rows:
            strip[n, used:, :] = jnp.zeros((plan.in_rows - used, LANES), jnp.float32)
    for g in range(dirs):
        slope_x = raw[g, 0]
        slope_y = raw[g, 1]
        tall_a[:rows, :] = keep * (slope_x + slope_y)
        tall_b[:rows, :] = keep * (slope_x - slope_y)
        both, diff = tall_a[...], tall_b[...]
        shifted_c = pltpu.roll(diff + pltpu.roll(both, 1, 0), 1, 1)
        field = (shifted_c - (both + pltpu.roll(diff, 1, 0))) * in_grid
        for n in range(strips):
            lanes = slice(n * LANES, (n + 1) * LANES)
            strip[n, g * rows : (g + 1) * rows, :] = field[:rows, lanes]
            strip[n, (dirs + 1) * rows + g : (dirs + 1) * rows + g + 1, :] = field[
                rows : rows + 1, lanes
            ]
    turned = {}
    lane = lane_index()

    def turn(n, by):
        if (n, by) not in turned:
            turned[n, by] = pltpu.roll(strip[n], (-by) % LANES, 1)
        return turned[n, by]

    for t in range(plan.tiles):
        begin = margin - plan.side + t * plan.own
        by = begin % LANES
        for n in range(plan.lane_tiles):
            at = begin // LANES + n
            if by == 0:
                out[t, n] = strip[at]
            else:
                near = tall(lane < LANES - by, plan.in_rows)
                out[t, n] = jnp.where(near, turn(at, by), turn(at + 1, by))


def solve_kernel(
    plan, place, offsets, weights, fields, out, q, keep, v0, v1, v2, phase, both, diff, smooth
):
    layers, dirs, rows = plan.layers, plan.dirs, plan.rows
    total, tiles = plan.grid_rows, range(plan.lane_tiles)
    chunk = total
    while chunk * plan.lane_tiles > 8 * 24:
        chunk //= 2
    starts = range(0, total, chunk)
    first = (place[0] * plan.tiles + place[1]) * plan.own - plan.side
    lane = lane_index()
    in_grid = []
    owned = []
    for t in tiles:
        local = lane + t * LANES
        column = local + first
        in_grid.append(
            tall(jnp.where((column >= 0) & (column < plan.width), 1.0, 0.0), chunk)
        )
        owned.append(tall((local >= plan.side) & (local < plan.side + plan.own), chunk))

    edge = jnp.zeros((PAD, LANES), jnp.float32)
    for t in tiles:
        for ref, count in ((q, dirs), (v0, layers), (v1, layers)):
            for i in range(count):
                ref[i, t, :PAD, :] = edge
                ref[i, t, PAD + total :, :] = edge
        for ref in (phase, both, diff, smooth):
            ref[t, :PAD, :] = edge
            ref[t, PAD + total :, :] = edge
        for s in range(plan.tiles):
            low = s * rows
            keep[t, low : low + rows, :] = fields[s, t, dirs * rows : (dirs + 1) * rows, :]
            for g in range(dirs):
                q[g, t, PAD + low : PAD + low + rows, :] = fields[s, t, g * rows : (g + 1) * rows, :]
        for s in range(1, plan.tiles):
            low = PAD + s * rows
            for g in range(dirs):
                carry = (dirs + 1) * rows + g
                q[g, t, low : low + 1, :] += fields[s - 1, t, carry : carry + 1, :]

    def back_project(layer, target, source):
        if source is not None:
            weight = weights[layer]
            for r in starts:
                x = [source[layer, t, PAD + r : PAD + r + chunk, :] for t in tiles]
                right = lane_shift(x, 1, chunk)
                left = lane_shift(x, -1, chunk)
                for t in tiles:
                    up = source[layer, t, PAD + r - 1 : PAD + r - 1 + chunk, :]
                    down = source[layer, t, PAD + r + 1 : PAD + r + 1 + chunk, :]
                    value = 4.0 * x[t] - up - down - left[t] - right[t]
                    smooth[t, PAD + r : PAD + r + chunk, :] = value * in_grid[t]
        for r in starts:
            sums = [jnp.zeros((chunk, LANES), jnp.float32) for _ in tiles]
            for g in range(dirs):
                at = (g * layers + layer) * 2
                low = PAD + r - offsets[at]
                moved = lane_shift(
                    [q[g, t, pl.ds(low, chunk), :] for t in tiles], -offsets[at + 1], chunk
                )
                sums = [sums[t] + moved[t] for t in tiles]
            sums = [0.5 * value for value in sums]
            if source is not None:
                x = [smooth[t, PAD + r : PAD + r + chunk, :] for t in tiles]
                right = lane_shift(x, 1, chunk)
                left = lane_shift(x, -1, chunk)
                for t in tiles:
                    up = smooth[t, PAD + r - 1 : PAD + r - 1 + chunk, :]
                    down = smooth[t, PAD + r + 1 : PAD + r + 1 + chunk, :]
                    value = 4.0 * x[t] - up - down - left[t] - right[t]
                    sums[t] = sums[t] + weight * value
            for t in tiles:
                target[layer, t, PAD + r : PAD + r + chunk, :] = sums[t] * in_grid[t]

    def project(g, source):
        for r in starts:
            sums = [jnp.zeros((chunk, LANES), jnp.float32) for _ in tiles]
            for layer in range(layers):
                at = (g * layers + layer) * 2
                low = PAD + r + offsets[at]
                moved = lane_shift(
                    [source[layer, t, pl.ds(low, chunk), :] for t in tiles], offsets[at + 1], chunk
                )
                sums = [sums[t] + moved[t] for t in tiles]
            for t in tiles:
                phase[t, PAD + r : PAD + r + chunk, :] = sums[t] * in_grid[t]
        for r in starts:
            p00 = [phase[t, PAD + r : PAD + r + chunk, :] for t in tiles]
            p10 = [phase[t, PAD + r + 1 : PAD + r + 1 + chunk, :] for t in tiles]
            p01 = lane_shift(p00, 1, chunk)
            p11 = lane_shift(p10, 1, chunk)
            for t in tiles:
                mask = keep[t, r : r + chunk, :]
                both[t, PAD + r : PAD + r + chunk, :] = mask * (p11[t] - p00[t])
                diff[t, PAD + r : PAD + r + chunk, :] = mask * (p01[t] - p10[t])
        for r in starts:
            here = slice(PAD + r, PAD + r + chunk)
            above = slice(PAD + r - 1, PAD + r - 1 + chunk)
            c = [diff[t, here, :] + both[t, above, :] for t in tiles]
            c = lane_shift(c, -1, chunk)
            for t in tiles:
                value = c[t] - (both[t, here, :] + diff[t, above, :])
                q[g, t, here, :] = value * in_grid[t]

    def each(count, body):
        def step(i, carry):
            body(i)
            return carry

        lax.fori_loop(0, count, step, 0)

    def fold(value):
        return jnp.sum(value.reshape(chunk // 8, 8, LANES), axis=0)

    def inner(terms, count):
        def step(layer, sums):
            for r in starts:
                for t in tiles:
                    pairs = terms(layer, t, slice(PAD + r, PAD + r + chunk))
                    sums = tuple(
                        s + fold(jnp.where(owned[t], value, 0.0)) for s, value in zip(sums, pairs)
                    )
            return sums

        zero = jnp.zeros((8, LANES), jnp.float32)
        sums = lax.fori_loop(0, layers, step, (zero,) * count)
        return [jnp.sum(s, keepdims=True) for s in sums]

    each(layers, lambda layer: back_project(layer, v0, None))
    each(dirs, lambda g: project(g, v0))
    each(layers, lambda layer: back_project(layer, v1, v0))

    def first_terms(layer, t, here):
        a, b = v0[layer, t, here, :], v1[layer, t, here, :]
        return a * a, a * b, b * b

    s00, s01, s11 = inner(first_terms, 3)
    coefficient = jnp.where(s11 > 0.0, s01 / jnp.where(s11 > 0.0, s11, 1.0), 0.0)
    each(dirs, lambda g: project(g, v1))
    each(layers, lambda layer: back_project(layer, v2, v1))
    spread = jnp.broadcast_to(coefficient, (chunk, LANES))

    def second_terms(layer, t, here):
        a, b, c = v0[layer, t, here, :], v1[layer, t, here, :], v2[layer, t, here, :]
        e = a - spread * b
        f = b - spread * c
        return e * e, e * b, e * f, e * c + b * f, b * c

    more = inner(second_terms, 5)
    scalars = [s00, s01, s11, coefficient] + more
    row = jnp.zeros((1, LANES), jnp.float32)
    for i, value in enumerate(scalars):
        row = jnp.where(lane[:1] == i, value, row)

    tail = 3 * plan.own_layers * rows
    note = jnp.broadcast_to(row[:, : plan.own], (plan.out_rows - tail, plan.own))
    keep_lanes = plan.side // LANES
    by = plan.side % LANES
    near = tall(lane < LANES - by, rows)
    for device in range(plan.layer_devices):
        for s in range(plan.tiles):
            to = device * plan.tiles + s
            for own in range(plan.own_layers):
                layer = device * plan.own_layers + own
                for i, ref in enumerate((v0, v1, v2)):
                    low = PAD + s * rows
                    block = [
                        pltpu.roll(ref[layer, t, low : low + rows, :], (-by) % LANES, 1)
                        for t in range(keep_lanes, plan.lane_tiles)
                    ]
                    pieces = []
                    for n in range(-(-plan.own // LANES)):
                        piece = block[n]
                        if n + 1 < len(block):
                            piece = jnp.where(near, piece, block[n + 1])
                        pieces.append(piece)
                    at = (own * 3 + i) * rows
                    for n, piece in enumerate(pieces):
                        size = min(LANES, plan.own - n * LANES)
                        out[to, at : at + rows, n * LANES : n * LANES + size] = piece[:, :size]
            out[to, tail:, :] = note


def coefficients(notes):
    s00, s01, s11, c, ee, eb, ef, mixed, bc = [notes[:, i : i + 1] for i in range(9)]

    def total(value):
        return jnp.sum(value, axis=0, keepdims=True)

    norm_0 = total(s00)
    power_0 = total(s01)
    alpha_0 = norm_0 / power_0
    delta = alpha_0 - c
    norm_1 = total(ee - 2.0 * delta * eb + delta * delta * s11)
    beta = norm_1 / norm_0
    power_1 = (
        total(ef - delta * mixed + delta * delta * bc)
        + 2.0 * beta * total(eb - delta * s11)
        + beta * beta * power_0
    )
    return alpha_0, beta, norm_1 / power_1


def outputs(a, b, c, scalars):
    alpha_0, beta, alpha_1 = scalars
    residual = a - alpha_0 * b
    image = b - alpha_0 * c
    estimate = alpha_0 * a + alpha_1 * (residual + beta * a)
    return estimate, residual - alpha_1 * (image + beta * b)


def combine_kernel(plan, blocks, estimate, residual):
    rows = plan.rows
    tail = 3 * plan.own_layers * rows
    scalars = coefficients(blocks[:, tail, :])
    scalars = [jnp.broadcast_to(value, (rows, plan.own)) for value in scalars]
    for k in range(plan.devices):
        for own in range(plan.own_layers):
            a, b, c = [
                blocks[k, (own * 3 + i) * rows : (own * 3 + i + 1) * rows, :] for i in range(3)
            ]
            x, r = outputs(a, b, c, scalars)
            estimate[own, :, k * plan.own : (k + 1) * plan.own] = x
            residual[own, :, k * plan.own : (k + 1) * plan.own] = r


def combine(plan, blocks):
    shape = (plan.own_layers, plan.rows, plan.width)
    if plan.own % LANES == 0:
        return pl.pallas_call(
            functools.partial(combine_kernel, plan),
            out_shape=[jax.ShapeDtypeStruct(shape, jnp.float32)] * 2,
            in_specs=[pl.BlockSpec(memory_space=VMEM)],
            out_specs=[pl.BlockSpec(memory_space=VMEM)] * 2,
            name="combine",
        )(blocks)
    tail = 3 * plan.own_layers * plan.rows
    scalars = coefficients(blocks[:, tail, :])
    fields = blocks[:, :tail].reshape(plan.devices, plan.own_layers, 3, plan.rows, plan.own)
    fields = fields.transpose(2, 1, 3, 0, 4).reshape((3,) + shape)
    return outputs(*fields, [value[0, 0] for value in scalars])


def per_device(mesh, measured_slopes, valid_mask, layer_offsets, reg_weight):
    dirs, _, rows, width = measured_slopes.shape
    plan = Plan(mesh, dirs, rows, width, reg_weight.shape[0])
    place = jnp.stack([lax.axis_index("layer"), lax.axis_index("tile")]).astype(jnp.int32)
    high = 16 * (-(-(rows + 1) // 16))
    strips = plan.strip // LANES
    sent = pl.pallas_call(
        functools.partial(gather_kernel, plan),
        out_shape=jax.ShapeDtypeStruct(
            (plan.tiles, plan.lane_tiles, plan.in_rows, LANES), jnp.float32
        ),
        in_specs=[
            pl.BlockSpec(memory_space=SMEM),
            pl.BlockSpec(memory_space=pl.ANY),
            pl.BlockSpec(memory_space=pl.ANY),
        ],
        out_specs=pl.BlockSpec(memory_space=VMEM),
        scratch_shapes=[
            pltpu.VMEM((dirs, 2, rows, plan.strip), jnp.float32),
            pltpu.VMEM((rows, plan.strip), jnp.int32),
            pltpu.VMEM((high, plan.strip), jnp.float32),
            pltpu.VMEM((high, plan.strip), jnp.float32),
            pltpu.VMEM((strips, plan.in_rows, LANES), jnp.float32),
            pltpu.SemaphoreType.DMA((2,)),
        ],
        name="gather",
    )(place, measured_slopes, valid_mask)
    fields = lax.all_to_all(sent, "tile", 0, 0)
    tall_rows = plan.grid_rows + 2 * PAD
    stack = pltpu.VMEM((plan.layers, plan.lane_tiles, tall_rows, LANES), jnp.float32)
    single = pltpu.VMEM((plan.lane_tiles, tall_rows, LANES), jnp.float32)
    blocks = pl.pallas_call(
        functools.partial(solve_kernel, plan),
        out_shape=jax.ShapeDtypeStruct((plan.devices, plan.out_rows, plan.own), jnp.float32),
        in_specs=[pl.BlockSpec(memory_space=SMEM)] * 3 + [pl.BlockSpec(memory_space=VMEM)],
        out_specs=pl.BlockSpec(memory_space=VMEM),
        scratch_shapes=[
            pltpu.VMEM((dirs, plan.lane_tiles, tall_rows, LANES), jnp.float32),
            pltpu.VMEM((plan.lane_tiles, plan.grid_rows, LANES), jnp.float32),
            stack,
            stack,
            stack,
            single,
            single,
            single,
            single,
        ],
        name="solve",
    )(place, layer_offsets.reshape(-1), reg_weight, fields)
    blocks = lax.all_to_all(blocks, ("layer", "tile"), 0, 0)
    return tuple(combine(plan, blocks))


def solution(mesh):
    return jax.shard_map(
        functools.partial(per_device, mesh),
        mesh=mesh,
        in_specs=(P(None, None, "tile", None), P("tile", None), P(), P()),
        out_specs=(P("layer", "tile", None), P("layer", "tile", None)),
        check_vma=False,
    )
```

```python
import functools

import jax
import jax.numpy as jnp
from jax import lax
from jax.experimental import pallas as pl
from jax.experimental.pallas import tpu as pltpu
from jax.sharding import PartitionSpec as P

HALO = 8
LANES = 128
PAD = 8
REACH_ROW = 2 * (2 * HALO + 1)
REACH = REACH_ROW + HALO + 1
VMEM = pltpu.MemorySpace.VMEM
SMEM = pltpu.MemorySpace.SMEM


def round_up(value, unit):
    return -(-value // unit) * unit


class Plan:
    def __init__(self, mesh, dirs, rows, width, layers):
        self.layer_devices = mesh.shape["layer"]
        self.tiles = mesh.shape["tile"]
        self.devices = self.layer_devices * self.tiles
        self.dirs = dirs
        self.rows = rows
        self.width = width
        self.layers = layers
        self.own_layers = layers // self.layer_devices
        self.grid_rows = rows * self.tiles
        assert width % self.devices == 0 and layers % self.layer_devices == 0
        self.own = width // self.devices
        self.part = width // self.layer_devices
        assert self.part % LANES == 0
        self.lane_tiles = round_up(self.own + 2 * REACH, LANES) // LANES
        self.side = (self.lane_tiles * LANES - self.own) // 2
        self.margin = round_up(self.side + 1, LANES)
        self.strip = self.part + 2 * self.margin
        assert self.margin <= 4 * LANES and (2 * self.part // LANES) % 8 == 0
        self.raw_rows = 2 * self.part // LANES + 16
        self.high = round_up(rows + 1, 8)
        self.in_rows = round_up(dirs * (rows + 1) + rows, 8)
        self.out_rows = round_up(3 * self.own_layers * rows + 1, 8)
        self.chips = self.tiles // 2
        self.direct = self.tiles in (2, 4, 8) and self.own == LANES and self.lane_tiles == 2
        self.outs = self.chips if self.direct else 1
        self.sent_tiles = self.lane_tiles + 1 if self.direct else self.lane_tiles
        self.chunk = self.grid_rows
        while self.chunk * self.lane_tiles > 8 * 24:
            self.chunk //= 2


def in_vmem(value):
    return pltpu.with_memory_space_constraint(value, VMEM)


def lane_index():
    return lax.broadcasted_iota(jnp.int32, (8, LANES), 1)


def tall(mask, rows):
    return jnp.broadcast_to(mask[:1], (rows, LANES))


def lane_shift(tiles, steps, rows):
    count = len(tiles)
    if isinstance(steps, int):
        turn = (-steps) % LANES
    else:
        turn = jnp.where(steps > 0, LANES - steps, -steps)
    turned = [pltpu.roll(tile, turn, 1) for tile in tiles]
    if count == 1:
        return turned
    source = lane_index() + steps
    past = tall(source >= LANES, rows)
    before = tall(source < 0, rows)
    if count == 2:
        outside = past | before
        return [jnp.where(outside, turned[1 - t], turned[t]) for t in range(2)]
    return [
        jnp.where(
            past,
            turned[(t + 1) % count],
            jnp.where(before, turned[(t - 1) % count], turned[t]),
        )
        for t in range(count)
    ]


def place_of():
    return lax.axis_index("layer"), lax.axis_index("tile")


def gather_kernel(plan, slopes, mask, *refs):
    outs, (raw, raw_mask, strip, ready, sems, mask_sems) = refs[: plan.outs], refs[plan.outs :]
    layer, tile = place_of()
    rows, dirs, part = plan.rows, plan.dirs, plan.part
    last = plan.layer_devices - 1
    core = 2 * part // LANES
    start = pl.multiple_of(layer * core, 8)
    column = pl.multiple_of(layer * part, LANES)
    side = plan.margin

    def slope_copy(g, piece, source, size, target):
        return pltpu.make_async_copy(
            slopes.at[g, :, pl.ds(source, size), :],
            raw.at[g, pl.ds(0, rows), pl.ds(target, size), :],
            sems.at[g, piece],
        )

    def mask_copy(piece, source, size, target):
        return pltpu.make_async_copy(
            mask.at[:, pl.ds(source, size)],
            raw_mask.at[:, pl.ds(target, size)],
            mask_sems.at[piece],
        )

    def copies(piece):
        if piece == 0:
            return [mask_copy(0, column, part, side)] + [
                slope_copy(g, 0, start, core, 8) for g in range(dirs)
            ]
        if piece == 1:
            return [mask_copy(1, pl.multiple_of(column - side, LANES), side, 0)] + [
                slope_copy(g, 1, pl.multiple_of(start - 8, 8), 8, 0) for g in range(dirs)
            ]
        return [mask_copy(2, pl.multiple_of(column + part, LANES), side, side + part)] + [
            slope_copy(g, 2, pl.multiple_of(start + core, 8), 8, 8 + core) for g in range(dirs)
        ]

    def both_ways(act):
        for copy in copies(0):
            act(copy)

        @pl.when(layer > 0)
        def _():
            for copy in copies(1):
                act(copy)

        @pl.when(layer < last)
        def _():
            for copy in copies(2):
                act(copy)

    both_ways(lambda copy: copy.start())

    @pl.when(layer == 0)
    def _():
        raw_mask[:, :side] = jnp.zeros((rows, side), jnp.int32)

    @pl.when(layer == last)
    def _():
        raw_mask[:, side + part :] = jnp.zeros((rows, side), jnp.int32)

    both_ways(lambda copy: copy.wait())

    strips = plan.strip // LANES
    high = plan.high
    used = dirs * (rows + 1) + rows
    lane = lane_index()
    wrap = tall(lane == 0, high)
    blank = jnp.zeros((high - rows, LANES), jnp.float32)
    valid = []
    for n in range(strips):
        keep = raw_mask[:, n * LANES : (n + 1) * LANES].astype(jnp.float32)
        strip[n, dirs * rows : (dirs + 1) * rows, :] = keep
        if used < plan.in_rows:
            strip[n, used:, :] = jnp.zeros((plan.in_rows - used, LANES), jnp.float32)
        valid.append(jnp.concatenate([keep, blank], axis=0) > 0.0)
    for g in range(dirs):
        flat = raw.at[g].reshape(high * plan.raw_rows, LANES)
        before = None
        for n in range(strips):
            at = 2 * n + 8 - 2 * (side // LANES)
            slope_x = flat[pl.ds(at, high, stride=plan.raw_rows), :]
            slope_y = flat[pl.ds(at + 1, high, stride=plan.raw_rows), :]
            both = jnp.where(valid[n], slope_x + slope_y, 0.0)
            diff = jnp.where(valid[n], slope_x - slope_y, 0.0)
            c = pltpu.roll(diff + pltpu.roll(both, 1, 0), 1, 1)
            shifted = c if before is None else jnp.where(wrap, before, c)
            before = c
            field = shifted - (both + pltpu.roll(diff, 1, 0))
            if n >= strips - side // LANES:
                inside = column + n * LANES - side + lane < plan.width
                field = jnp.where(tall(inside, high), field, 0.0)
            strip[n, g * rows : (g + 1) * rows, :] = field[:rows]
            carry = (dirs + 1) * rows + g
            strip[n, carry : carry + 1, :] = field[rows : rows + 1]
    turned = {}

    def turn(n, by):
        if by == 0:
            return strip[n]
        for at in (n, n + 1):
            if (at, by) not in turned:
                turned[at, by] = pltpu.roll(strip[at], (-by) % LANES, 1)
        near = tall(lane < LANES - by, plan.in_rows)
        return jnp.where(near, turned[n, by], turned[n + 1, by])

    begin = plan.margin - plan.side
    if plan.direct:
        for n in range(2 * plan.chips + 1):
            ready[n] = turn(begin // LANES + n, begin % LANES)
        for k, out in enumerate(outs):
            at = 2 * ((tile // 2) ^ k)
            for n in range(plan.sent_tiles):
                out[n] = ready[at + n]
        return
    for t in range(plan.tiles):
        at = begin + t * plan.own
        for n in range(plan.lane_tiles):
            outs[0][t, n] = turn(at // LANES + n, at % LANES)


def solve_kernel(plan, offsets, weights, *refs):
    count = 2 * plan.outs if plan.direct else 1
    fields, (out, q, keep, v0, v1, phase, smooth, packed) = refs[:count], refs[count:]
    layers, dirs, rows = plan.layers, plan.dirs, plan.rows
    total, tiles = plan.grid_rows, range(plan.lane_tiles)
    chunk = plan.chunk
    starts = range(0, total, chunk)
    unrolled = len(starts) == 1
    layer_place, tile_place = place_of()
    first = (layer_place * plan.tiles + tile_place) * plan.own - plan.side
    lane = lane_index()
    in_grid = []
    owned = []
    for t in tiles:
        local = lane + t * LANES
        column = local + first
        in_grid.append(tall(jnp.where((column >= 0) & (column < plan.width), 1.0, 0.0), chunk))
        owned.append(tall((local >= plan.side) & (local < plan.side + plan.own), chunk))
    two = plan.lane_tiles == 2 and plan.own == LANES

    def pack(window):
        if two:
            return jnp.where(owned[1], window[1], window[0])
        value = jnp.where(owned[0], window[0], 0.0)
        for t in tiles[1:]:
            value = jnp.where(owned[t], window[t], value)
        return value

    def packed_shift(window, steps):
        if not two:
            return pack(lane_shift(window, steps, chunk))
        turn = jnp.where(steps > 0, LANES - steps, -steps)
        turned = [pltpu.roll(tile, turn, 1) for tile in window]
        source = lane + steps
        outside = (source >= LANES) | (source < 0)
        swap = tall(outside ^ (lane < plan.side), chunk)
        return jnp.where(swap, turned[1], turned[0])

    edge = jnp.zeros((PAD, LANES), jnp.float32)
    for t in tiles:
        for ref, count in ((q, dirs), (v0, layers), (v1, layers), (phase, dirs), (smooth, layers)):
            for i in range(count):
                for half in ([()] if ref is not phase else [(0,), (1,)]):
                    ref[(i,) + half + (t, slice(0, PAD))] = edge
                    ref[(i,) + half + (t, slice(PAD + total, PAD + total + PAD))] = edge
        keep[t, :PAD, :] = edge
        keep[t, PAD + total :, :] = edge
    sources = []
    if plan.direct:
        core = tile_place % 2
        for i, field in enumerate(fields):
            tile = 2 * ((tile_place // 2) ^ (i % plan.outs)) + (core if i < plan.outs else 1 - core)
            sources.append((tile, [field.at[core + t] for t in tiles]))
    else:
        for tile in range(plan.tiles):
            sources.append((tile, [fields[0].at[tile, t] for t in tiles]))
    for tile, windows in sources:
        here = pl.ds(PAD + tile * rows, rows)
        for t, window in enumerate(windows):
            keep[t, here, :] = window[dirs * rows : (dirs + 1) * rows, :]
            for g in range(dirs):
                q[g, t, here, :] = window[g * rows : (g + 1) * rows, :]
    for tile, windows in sources:
        below = pl.ds(PAD + (tile + 1) * rows, 1)
        counts = jnp.where(tile + 1 < plan.tiles, 1.0, 0.0)
        for t, window in enumerate(windows):
            for g in range(dirs):
                carry = (dirs + 1) * rows + g
                q[g, t, below, :] += window[carry : carry + 1, :] * counts

    def four(x, up, down, left, right):
        return 4.0 * x - (up + down) - (left + right)

    def back_project(layer, level):
        source = (None, v0, v1)[level]
        if source is not None:
            for r in starts:
                here = slice(PAD + r, PAD + r + chunk)
                x = [source[layer, t, here, :] for t in tiles]
                right = lane_shift(x, 1, chunk)
                left = lane_shift(x, -1, chunk)
                for t in tiles:
                    up = source[layer, t, PAD + r - 1 : PAD + r - 1 + chunk, :]
                    down = source[layer, t, PAD + r + 1 : PAD + r + 1 + chunk, :]
                    smooth[layer, t, here, :] = four(x[t], up, down, left[t], right[t]) * in_grid[t]
        for r in starts:
            here = slice(PAD + r, PAD + r + chunk)
            sums = None
            for g in range(dirs):
                at = (g * layers + layer) * 2
                low = PAD + r - offsets[at]
                window = [q[g, t, pl.ds(low, chunk), :] for t in tiles]
                if level == 2:
                    moved = [packed_shift(window, -offsets[at + 1])]
                else:
                    moved = lane_shift(window, -offsets[at + 1], chunk)
                sums = moved if sums is None else [s + m for s, m in zip(sums, moved)]
            sums = [0.5 * value for value in sums]
            if source is not None:
                weight = weights[layer]
                x = [smooth[layer, t, here, :] for t in tiles]
                right = lane_shift(x, 1, chunk)
                left = lane_shift(x, -1, chunk)
                lap = []
                for t in tiles:
                    up = smooth[layer, t, PAD + r - 1 : PAD + r - 1 + chunk, :]
                    down = smooth[layer, t, PAD + r + 1 : PAD + r + 1 + chunk, :]
                    lap.append(four(x[t], up, down, left[t], right[t]))
                if level == 2:
                    lap = [pack(lap)]
                sums = [s + weight * value for s, value in zip(sums, lap)]
            if level == 2:
                packed[2, layer, r : r + chunk, :] = sums[0]
                continue
            sums = [s * inside for s, inside in zip(sums, in_grid)]
            target = (v0, v1)[level]
            for t in tiles:
                target[layer, t, here, :] = sums[t]
            packed[level, layer, r : r + chunk, :] = pack(sums)

    def project(g, source):
        for r in starts:
            here = slice(PAD + r, PAD + r + chunk)
            sums = None
            for layer in range(layers):
                at = (g * layers + layer) * 2
                low = PAD + r + offsets[at]
                window = [source[layer, t, pl.ds(low, chunk), :] for t in tiles]
                moved = lane_shift(window, offsets[at + 1], chunk)
                sums = moved if sums is None else [s + m for s, m in zip(sums, moved)]
            sums = [s * inside for s, inside in zip(sums, in_grid)]
            right = lane_shift(sums, 1, chunk)
            for t in tiles:
                phase[g, 0, t, here, :] = sums[t]
                phase[g, 1, t, here, :] = right[t]
        for r in starts:
            here = slice(PAD + r, PAD + r + chunk)
            below = slice(PAD + r + 1, PAD + r + 1 + chunk)
            above = slice(PAD + r - 1, PAD + r - 1 + chunk)
            ahead, level = [], []
            for t in tiles:
                p00, p01 = phase[g, 0, t, here, :], phase[g, 1, t, here, :]
                p10, p11 = phase[g, 0, t, below, :], phase[g, 1, t, below, :]
                up0, up1 = phase[g, 0, t, above, :], phase[g, 1, t, above, :]
                mask, mask_up = keep[t, here, :], keep[t, above, :]
                ahead.append(mask * (p01 - p10) + mask_up * (p01 - up0))
                level.append(mask * (p11 - p00) + mask_up * (up1 - p00))
            ahead = lane_shift(ahead, -1, chunk)
            for t in tiles:
                q[g, t, here, :] = (ahead[t] - level[t]) * in_grid[t]

    def each(count, body):
        if unrolled:
            for i in range(count):
                body(i)
            return

        def step(i, carry):
            body(i)
            return carry

        lax.fori_loop(0, count, step, 0)

    def fold(value):
        return jnp.sum(value.reshape(chunk // 8, 8, LANES), axis=0)

    def inner(terms, count):
        sums = [jnp.zeros((8, LANES), jnp.float32)] * count

        def step(layer, sums):
            for r in starts:
                values = terms([packed.at[i, layer, r : r + chunk, :] for i in range(3)])
                sums = [s + fold(value) for s, value in zip(sums, values)]
            return tuple(sums)

        if unrolled:
            for layer in range(layers):
                sums = step(layer, sums)
        else:
            sums = lax.fori_loop(0, layers, step, tuple(sums))
        return [jnp.sum(s, keepdims=True) for s in sums]

    def first_terms(refs):
        a, b = refs[0][...], refs[1][...]
        return a * a, a * b, b * b

    each(layers, lambda layer: back_project(layer, 0))
    each(dirs, lambda g: project(g, v0))
    each(layers, lambda layer: back_project(layer, 1))
    s00, s01, s11 = inner(first_terms, 3)
    coefficient = jnp.where(s11 > 0.0, s01 / jnp.where(s11 > 0.0, s11, 1.0), 0.0)
    each(dirs, lambda g: project(g, v1))
    each(layers, lambda layer: back_project(layer, 2))
    spread = jnp.broadcast_to(coefficient, (chunk, LANES))

    def second_terms(refs):
        a, b, c = [ref[...] for ref in refs]
        e = a - spread * b
        f = b - spread * c
        return e * e, e * b, e * f, e * c + b * f, b * c

    scalars = [s00, s01, s11, coefficient] + inner(second_terms, 5)
    row = jnp.zeros((1, LANES), jnp.float32)
    for i, value in enumerate(scalars):
        row = jnp.where(lane[:1] == i, value, row)
    tail = 3 * plan.own_layers * rows
    note = jnp.broadcast_to(row[:, : plan.own], (plan.out_rows - tail, plan.own))
    for device in range(plan.layer_devices):
        for s in range(plan.tiles):
            to = device * plan.tiles + s
            for own in range(plan.own_layers):
                for i in range(3):
                    block = packed[i, device * plan.own_layers + own, s * rows : (s + 1) * rows, :]
                    if plan.own < LANES:
                        block = pltpu.roll(block, (-plan.side) % LANES, 1)[:, : plan.own]
                    at = (own * 3 + i) * rows
                    out[to, at : at + rows, :] = block
            out[to, tail:, :] = note


def coefficients(notes):
    s00, s01, s11, c, ee, eb, ef, mixed, bc = [notes[:, i : i + 1] for i in range(9)]

    def total(value):
        return jnp.sum(value, axis=0, keepdims=True)

    norm_0 = total(s00)
    power_0 = total(s01)
    alpha_0 = norm_0 / power_0
    delta = alpha_0 - c
    norm_1 = total(ee - 2.0 * delta * eb + delta * delta * s11)
    beta = norm_1 / norm_0
    power_1 = (
        total(ef - delta * mixed + delta * delta * bc)
        + 2.0 * beta * total(eb - delta * s11)
        + beta * beta * power_0
    )
    return alpha_0, beta, norm_1 / power_1


def outputs(a, b, c, scalars):
    alpha_0, beta, alpha_1 = scalars
    residual = a - alpha_0 * b
    image = b - alpha_0 * c
    estimate = alpha_0 * a + alpha_1 * (residual + beta * a)
    return estimate, residual - alpha_1 * (image + beta * b)


def combine_kernel(plan, blocks, estimate, residual):
    rows = plan.rows
    tail = 3 * plan.own_layers * rows
    scalars = coefficients(blocks[:, tail, :])
    scalars = [jnp.broadcast_to(value, (rows, LANES)) for value in scalars]
    for k in range(plan.devices):
        for own in range(plan.own_layers):
            a, b, c = [
                blocks[k, (own * 3 + i) * rows : (own * 3 + i + 1) * rows, :] for i in range(3)
            ]
            where = pl.ds(own * rows * plan.devices + k, rows, stride=plan.devices)
            for value, ref in zip(outputs(a, b, c, scalars), (estimate, residual)):
                ref[where, :] = pltpu.roll(value, (-plan.side) % LANES, 1)


def combine(plan, blocks):
    shape = (plan.own_layers, plan.rows, plan.width)
    if plan.own == LANES:
        lines = (plan.own_layers * plan.rows * plan.devices, LANES)
        results = pl.pallas_call(
            functools.partial(combine_kernel, plan),
            out_shape=[jax.ShapeDtypeStruct(lines, jnp.float32)] * 2,
            in_specs=[pl.BlockSpec(memory_space=VMEM)],
            out_specs=[pl.BlockSpec(memory_space=VMEM)] * 2,
            name="combine",
        )(in_vmem(blocks))
        return [value.reshape(shape) for value in results]
    tail = 3 * plan.own_layers * plan.rows
    scalars = coefficients(blocks[:, tail, :])
    fields = blocks[:, :tail].reshape(plan.devices, plan.own_layers, 3, plan.rows, plan.own)
    fields = fields.transpose(2, 1, 3, 0, 4).reshape((3,) + shape)
    return outputs(*fields, [value[0, 0] for value in scalars])


def per_device(mesh, measured_slopes, valid_mask, layer_offsets, reg_weight):
    dirs, _, rows, width = measured_slopes.shape
    plan = Plan(mesh, dirs, rows, width, reg_weight.shape[0])
    column_tiles = width // LANES
    slopes = measured_slopes.reshape(dirs, 2, rows, column_tiles, LANES)
    slopes = slopes.transpose(0, 2, 3, 1, 4).reshape(dirs, rows, 2 * column_tiles, LANES)
    strips = plan.strip // LANES
    piece = (plan.sent_tiles, plan.in_rows, LANES)
    lead = () if plan.direct else (plan.tiles,)
    sent = pl.pallas_call(
        functools.partial(gather_kernel, plan),
        out_shape=[jax.ShapeDtypeStruct(lead + piece, jnp.float32)] * plan.outs,
        in_specs=[pl.BlockSpec(memory_space=pl.ANY)] * 2,
        out_specs=[pl.BlockSpec(memory_space=VMEM)] * plan.outs,
        scratch_shapes=[
            pltpu.VMEM((dirs, plan.high, plan.raw_rows, LANES), jnp.float32),
            pltpu.VMEM((rows, plan.strip), jnp.int32),
            pltpu.VMEM((strips, plan.in_rows, LANES), jnp.float32),
            pltpu.VMEM((strips - 1, plan.in_rows, LANES), jnp.float32),
            pltpu.SemaphoreType.DMA((dirs, 3)),
            pltpu.SemaphoreType.DMA((3,)),
        ],
        name="gather",
    )(slopes, valid_mask)
    if plan.direct:
        fields = list(sent)
        for k in reversed(range(1, plan.outs)):
            fields[k] = lax.ppermute(sent[k], "tile", [(i, i ^ (2 * k)) for i in range(plan.tiles)])
        swap = [(i, i ^ 1) for i in range(plan.tiles)]
        fields = fields + [lax.ppermute(field, "tile", swap) for field in fields]
    else:
        fields = [lax.all_to_all(sent[0], "tile", 0, 0)]
    fields = [in_vmem(field) for field in fields]
    tall_rows = plan.grid_rows + 2 * PAD

    def scratch(*lead):
        return pltpu.VMEM(lead + (plan.lane_tiles, tall_rows, LANES), jnp.float32)

    blocks = pl.pallas_call(
        functools.partial(solve_kernel, plan),
        out_shape=jax.ShapeDtypeStruct((plan.devices, plan.out_rows, plan.own), jnp.float32),
        in_specs=[pl.BlockSpec(memory_space=SMEM)] * 2
        + [pl.BlockSpec(memory_space=VMEM)] * len(fields),
        out_specs=pl.BlockSpec(memory_space=VMEM),
        scratch_shapes=[
            scratch(dirs),
            scratch(),
            scratch(plan.layers),
            scratch(plan.layers),
            scratch(dirs, 2),
            scratch(plan.layers),
            pltpu.VMEM((3, plan.layers, plan.grid_rows, LANES), jnp.float32),
        ],
        name="solve",
    )(layer_offsets.reshape(-1), reg_weight, *fields)
    blocks = lax.all_to_all(blocks, ("layer", "tile"), 0, 0)
    return tuple(combine(plan, blocks))


def solution(mesh):
    return jax.shard_map(
        functools.partial(per_device, mesh),
        mesh=mesh,
        in_specs=(P(None, None, "tile", None), P("tile", None), P(), P()),
        out_specs=(P("layer", "tile", None), P("layer", "tile", None)),
        check_vma=False,
    )
```

```python
import functools

import jax
import jax.numpy as jnp
from jax import lax
from jax.experimental import pallas as pl
from jax.experimental.pallas import tpu as pltpu
from jax.sharding import PartitionSpec as P

HALO = 8
LANES = 128
PAD = 8
REACH_ROW = 2 * (2 * HALO + 1)
REACH = REACH_ROW + HALO + 1
VMEM = pltpu.MemorySpace.VMEM
SMEM = pltpu.MemorySpace.SMEM


def round_up(value, unit):
    return -(-value // unit) * unit


class Plan:
    def __init__(self, mesh, dirs, rows, width, layers):
        self.layer_devices = mesh.shape["layer"]
        self.tiles = mesh.shape["tile"]
        self.devices = self.layer_devices * self.tiles
        self.dirs = dirs
        self.rows = rows
        self.width = width
        self.layers = layers
        self.own_layers = layers // self.layer_devices
        self.grid_rows = rows * self.tiles
        assert width % self.devices == 0 and layers % self.layer_devices == 0
        self.own = width // self.devices
        self.part = width // self.layer_devices
        assert self.part % LANES == 0
        self.lane_tiles = round_up(self.own + 2 * REACH, LANES) // LANES
        self.side = (self.lane_tiles * LANES - self.own) // 2
        self.margin = round_up(self.side + 1, LANES)
        self.strip = self.part + 2 * self.margin
        assert self.margin <= 4 * LANES and (2 * self.part // LANES) % 8 == 0
        self.raw_rows = 2 * self.part // LANES + 16
        self.high = round_up(rows + 1, 8)
        self.in_rows = round_up(dirs * (rows + 1) + rows, 8)
        self.out_rows = round_up(3 * self.own_layers * rows + 1, 8)
        self.chips = self.tiles // 2
        self.direct = self.tiles in (2, 4, 8) and self.own == LANES and self.lane_tiles == 2
        self.outs = self.chips if self.direct else 1
        self.sent_tiles = self.lane_tiles + 1 if self.direct else self.lane_tiles
        self.chunk = self.grid_rows
        while self.chunk * self.lane_tiles > 8 * 24:
            self.chunk //= 2


def in_vmem(value):
    return pltpu.with_memory_space_constraint(value, VMEM)


def lane_index():
    return lax.broadcasted_iota(jnp.int32, (8, LANES), 1)


def tall(mask, rows):
    return jnp.broadcast_to(mask[:1], (rows, LANES))


def lane_shift(tiles, steps, rows):
    count = len(tiles)
    if isinstance(steps, int):
        turn = (-steps) % LANES
    else:
        turn = jnp.where(steps > 0, LANES - steps, -steps)
    turned = [pltpu.roll(tile, turn, 1) for tile in tiles]
    if count == 1:
        return turned
    source = lane_index() + steps
    past = tall(source >= LANES, rows)
    before = tall(source < 0, rows)
    if count == 2:
        outside = past | before
        return [jnp.where(outside, turned[1 - t], turned[t]) for t in range(2)]
    return [
        jnp.where(
            past,
            turned[(t + 1) % count],
            jnp.where(before, turned[(t - 1) % count], turned[t]),
        )
        for t in range(count)
    ]


def place_of():
    return lax.axis_index("layer"), lax.axis_index("tile")


def gather_kernel(plan, slopes, mask, *refs):
    outs, (raw, raw_mask, strip, ready, sems, mask_sems) = refs[: plan.outs], refs[plan.outs :]
    layer, tile = place_of()
    rows, dirs, part = plan.rows, plan.dirs, plan.part
    last = plan.layer_devices - 1
    core = 2 * part // LANES
    start = pl.multiple_of(layer * core, 8)
    column = pl.multiple_of(layer * part, LANES)
    side = plan.margin

    def slope_copy(g, piece, source, size, target):
        return pltpu.make_async_copy(
            slopes.at[g, :, pl.ds(source, size), :],
            raw.at[g, pl.ds(0, rows), pl.ds(target, size), :],
            sems.at[g, piece],
        )

    def mask_copy(piece, source, size, target):
        return pltpu.make_async_copy(
            mask.at[:, pl.ds(source, size)],
            raw_mask.at[:, pl.ds(target, size)],
            mask_sems.at[piece],
        )

    def copies(piece):
        if piece == 0:
            return [mask_copy(0, column, part, side)] + [
                slope_copy(g, 0, start, core, 8) for g in range(dirs)
            ]
        if piece == 1:
            return [mask_copy(1, pl.multiple_of(column - side, LANES), side, 0)] + [
                slope_copy(g, 1, pl.multiple_of(start - 8, 8), 8, 0) for g in range(dirs)
            ]
        return [mask_copy(2, pl.multiple_of(column + part, LANES), side, side + part)] + [
            slope_copy(g, 2, pl.multiple_of(start + core, 8), 8, 8 + core) for g in range(dirs)
        ]

    def both_ways(act):
        for copy in copies(0):
            act(copy)

        @pl.when(layer > 0)
        def _():
            for copy in copies(1):
                act(copy)

        @pl.when(layer < last)
        def _():
            for copy in copies(2):
                act(copy)

    both_ways(lambda copy: copy.start())

    @pl.when(layer == 0)
    def _():
        raw_mask[:, :side] = jnp.zeros((rows, side), jnp.int32)

    @pl.when(layer == last)
    def _():
        raw_mask[:, side + part :] = jnp.zeros((rows, side), jnp.int32)

    both_ways(lambda copy: copy.wait())

    strips = plan.strip // LANES
    high = plan.high
    used = dirs * (rows + 1) + rows
    lane = lane_index()
    wrap = tall(lane == 0, high)
    blank = jnp.zeros((high - rows, LANES), jnp.float32)
    valid = []
    for n in range(strips):
        keep = raw_mask[:, n * LANES : (n + 1) * LANES].astype(jnp.float32)
        strip[n, dirs * rows : (dirs + 1) * rows, :] = keep
        if used < plan.in_rows:
            strip[n, used:, :] = jnp.zeros((plan.in_rows - used, LANES), jnp.float32)
        valid.append(jnp.concatenate([keep, blank], axis=0) > 0.0)
    for g in range(dirs):
        flat = raw.at[g].reshape(high * plan.raw_rows, LANES)
        before = None
        for n in range(strips):
            at = 2 * n + 8 - 2 * (side // LANES)
            slope_x = flat[pl.ds(at, high, stride=plan.raw_rows), :]
            slope_y = flat[pl.ds(at + 1, high, stride=plan.raw_rows), :]
            both = jnp.where(valid[n], slope_x + slope_y, 0.0)
            diff = jnp.where(valid[n], slope_x - slope_y, 0.0)
            c = pltpu.roll(diff + pltpu.roll(both, 1, 0), 1, 1)
            shifted = c if before is None else jnp.where(wrap, before, c)
            before = c
            field = shifted - (both + pltpu.roll(diff, 1, 0))
            if n >= strips - side // LANES:
                inside = column + n * LANES - side + lane < plan.width
                field = jnp.where(tall(inside, high), field, 0.0)
            strip[n, g * rows : (g + 1) * rows, :] = field[:rows]
            carry = (dirs + 1) * rows + g
            strip[n, carry : carry + 1, :] = field[rows : rows + 1]
    turned = {}

    def turn(n, by):
        if by == 0:
            return strip[n]
        for at in (n, n + 1):
            if (at, by) not in turned:
                turned[at, by] = pltpu.roll(strip[at], (-by) % LANES, 1)
        near = tall(lane < LANES - by, plan.in_rows)
        return jnp.where(near, turned[n, by], turned[n + 1, by])

    begin = plan.margin - plan.side
    if plan.direct:
        for n in range(2 * plan.chips + 1):
            ready[n] = turn(begin // LANES + n, begin % LANES)
        for k, out in enumerate(outs):
            at = 2 * ((tile // 2) ^ k)
            for n in range(plan.sent_tiles):
                out[n] = ready[at + n]
        return
    for t in range(plan.tiles):
        at = begin + t * plan.own
        for n in range(plan.lane_tiles):
            outs[0][t, n] = turn(at // LANES + n, at % LANES)


def solve_kernel(plan, offsets, weights, *refs):
    count = 2 * plan.outs if plan.direct else 1
    fields, (out, q, keep, v0, v1, phase, smooth, packed) = refs[:count], refs[count:]
    layers, dirs, rows = plan.layers, plan.dirs, plan.rows
    total, tiles = plan.grid_rows, range(plan.lane_tiles)
    chunk = plan.chunk
    starts = range(0, total, chunk)
    unrolled = len(starts) == 1
    layer_place, tile_place = place_of()
    first = (layer_place * plan.tiles + tile_place) * plan.own - plan.side
    lane = lane_index()
    in_grid = []
    owned = []
    for t in tiles:
        local = lane + t * LANES
        column = local + first
        in_grid.append(tall(jnp.where((column >= 0) & (column < plan.width), 1.0, 0.0), chunk))
        owned.append(tall((local >= plan.side) & (local < plan.side + plan.own), chunk))
    two = plan.lane_tiles == 2 and plan.own == LANES

    def pack(window):
        if two:
            return jnp.where(owned[1], window[1], window[0])
        value = jnp.where(owned[0], window[0], 0.0)
        for t in tiles[1:]:
            value = jnp.where(owned[t], window[t], value)
        return value

    def packed_shift(window, steps):
        if not two:
            return pack(lane_shift(window, steps, chunk))
        turn = jnp.where(steps > 0, LANES - steps, -steps)
        turned = [pltpu.roll(tile, turn, 1) for tile in window]
        source = lane + steps
        outside = (source >= LANES) | (source < 0)
        swap = tall(outside ^ (lane < plan.side), chunk)
        return jnp.where(swap, turned[1], turned[0])

    edge = jnp.zeros((PAD, LANES), jnp.float32)
    for t in tiles:
        for ref, count in ((q, dirs), (v0, layers), (v1, layers), (phase, dirs), (smooth, layers)):
            for i in range(count):
                for half in ([()] if ref is not phase else [(0,), (1,)]):
                    ref[(i,) + half + (t, slice(0, PAD))] = edge
                    ref[(i,) + half + (t, slice(PAD + total, PAD + total + PAD))] = edge
        keep[t, :PAD, :] = edge
        keep[t, PAD + total :, :] = edge
    sources = []
    if plan.direct:
        core = tile_place % 2
        for i, field in enumerate(fields):
            tile = 2 * ((tile_place // 2) ^ (i % plan.outs)) + (core if i < plan.outs else 1 - core)
            sources.append((tile, [field.at[core + t] for t in tiles]))
    else:
        for tile in range(plan.tiles):
            sources.append((tile, [fields[0].at[tile, t] for t in tiles]))
    for tile, windows in sources:
        here = pl.ds(PAD + tile * rows, rows)
        for t, window in enumerate(windows):
            keep[t, here, :] = window[dirs * rows : (dirs + 1) * rows, :]
            for g in range(dirs):
                q[g, t, here, :] = window[g * rows : (g + 1) * rows, :]
    for tile, windows in sources:
        below = pl.ds(PAD + (tile + 1) * rows, 1)
        counts = jnp.where(tile + 1 < plan.tiles, 1.0, 0.0)
        for t, window in enumerate(windows):
            for g in range(dirs):
                carry = (dirs + 1) * rows + g
                q[g, t, below, :] += window[carry : carry + 1, :] * counts

    def four(x, up, down, left, right):
        return 4.0 * x - (up + down) - (left + right)

    def back_project(layer, level):
        source = (None, v0, v1)[level]
        if source is not None:
            for r in starts:
                here = slice(PAD + r, PAD + r + chunk)
                x = [source[layer, t, here, :] for t in tiles]
                right = lane_shift(x, 1, chunk)
                left = lane_shift(x, -1, chunk)
                for t in tiles:
                    up = source[layer, t, PAD + r - 1 : PAD + r - 1 + chunk, :]
                    down = source[layer, t, PAD + r + 1 : PAD + r + 1 + chunk, :]
                    smooth[layer, t, here, :] = four(x[t], up, down, left[t], right[t]) * in_grid[t]
        for r in starts:
            here = slice(PAD + r, PAD + r + chunk)
            sums = None
            for g in range(dirs):
                low = PAD + r - offsets[layer, 0, g]
                window = [q[g, t, pl.ds(low, chunk), :] for t in tiles]
                if level == 2:
                    moved = [packed_shift(window, -offsets[layer, 1, g])]
                else:
                    moved = lane_shift(window, -offsets[layer, 1, g], chunk)
                sums = moved if sums is None else [s + m for s, m in zip(sums, moved)]
            sums = [0.5 * value for value in sums]
            if source is not None:
                weight = weights[layer]
                x = [smooth[layer, t, here, :] for t in tiles]
                right = lane_shift(x, 1, chunk)
                left = lane_shift(x, -1, chunk)
                lap = []
                for t in tiles:
                    up = smooth[layer, t, PAD + r - 1 : PAD + r - 1 + chunk, :]
                    down = smooth[layer, t, PAD + r + 1 : PAD + r + 1 + chunk, :]
                    lap.append(four(x[t], up, down, left[t], right[t]))
                if level == 2:
                    lap = [pack(lap)]
                sums = [s + weight * value for s, value in zip(sums, lap)]
            if level == 2:
                packed[2, layer, r : r + chunk, :] = sums[0]
                continue
            sums = [s * inside for s, inside in zip(sums, in_grid)]
            target = (v0, v1)[level]
            for t in tiles:
                target[layer, t, here, :] = sums[t]
            packed[level, layer, r : r + chunk, :] = pack(sums)

    def project(g, source):
        for r in starts:
            here = slice(PAD + r, PAD + r + chunk)
            sums = None
            for layer in range(layers):
                low = PAD + r + offsets[layer, 0, g]
                window = [source[layer, t, pl.ds(low, chunk), :] for t in tiles]
                moved = lane_shift(window, offsets[layer, 1, g], chunk)
                sums = moved if sums is None else [s + m for s, m in zip(sums, moved)]
            sums = [s * inside for s, inside in zip(sums, in_grid)]
            right = lane_shift(sums, 1, chunk)
            for t in tiles:
                phase[g, 0, t, here, :] = sums[t]
                phase[g, 1, t, here, :] = right[t]
        for r in starts:
            here = slice(PAD + r, PAD + r + chunk)
            below = slice(PAD + r + 1, PAD + r + 1 + chunk)
            above = slice(PAD + r - 1, PAD + r - 1 + chunk)
            ahead, level = [], []
            for t in tiles:
                p00, p01 = phase[g, 0, t, here, :], phase[g, 1, t, here, :]
                p10, p11 = phase[g, 0, t, below, :], phase[g, 1, t, below, :]
                up0, up1 = phase[g, 0, t, above, :], phase[g, 1, t, above, :]
                mask, mask_up = keep[t, here, :], keep[t, above, :]
                ahead.append(mask * (p01 - p10) + mask_up * (p01 - up0))
                level.append(mask * (p11 - p00) + mask_up * (up1 - p00))
            ahead = lane_shift(ahead, -1, chunk)
            for t in tiles:
                q[g, t, here, :] = (ahead[t] - level[t]) * in_grid[t]

    def each(count, body):
        if unrolled:
            for i in range(count):
                body(i)
            return

        def step(i, carry):
            body(i)
            return carry

        lax.fori_loop(0, count, step, 0)

    def fold(value):
        return jnp.sum(value.reshape(chunk // 8, 8, LANES), axis=0)

    def inner(terms, count):
        sums = [jnp.zeros((8, LANES), jnp.float32)] * count

        def step(layer, sums):
            for r in starts:
                values = terms([packed.at[i, layer, r : r + chunk, :] for i in range(3)])
                sums = [s + fold(value) for s, value in zip(sums, values)]
            return tuple(sums)

        if unrolled:
            for layer in range(layers):
                sums = step(layer, sums)
        else:
            sums = lax.fori_loop(0, layers, step, tuple(sums))
        return [jnp.sum(s, keepdims=True) for s in sums]

    def first_terms(refs):
        a, b = refs[0][...], refs[1][...]
        return a * a, a * b, b * b

    each(layers, lambda layer: back_project(layer, 0))
    each(dirs, lambda g: project(g, v0))
    each(layers, lambda layer: back_project(layer, 1))
    s00, s01, s11 = inner(first_terms, 3)
    coefficient = jnp.where(s11 > 0.0, s01 / jnp.where(s11 > 0.0, s11, 1.0), 0.0)
    each(dirs, lambda g: project(g, v1))
    each(layers, lambda layer: back_project(layer, 2))
    spread = jnp.broadcast_to(coefficient, (chunk, LANES))

    def second_terms(refs):
        a, b, c = [ref[...] for ref in refs]
        e = a - spread * b
        f = b - spread * c
        return e * e, e * b, e * f, e * c + b * f, b * c

    scalars = [s00, s01, s11, coefficient] + inner(second_terms, 5)
    row = jnp.zeros((1, LANES), jnp.float32)
    for i, value in enumerate(scalars):
        row = jnp.where(lane[:1] == i, value, row)
    tail = 3 * plan.own_layers * rows
    note = jnp.broadcast_to(row[:, : plan.own], (plan.out_rows - tail, plan.own))
    for device in range(plan.layer_devices):
        for s in range(plan.tiles):
            to = device * plan.tiles + s
            for own in range(plan.own_layers):
                for i in range(3):
                    block = packed[i, device * plan.own_layers + own, s * rows : (s + 1) * rows, :]
                    if plan.own < LANES:
                        block = pltpu.roll(block, (-plan.side) % LANES, 1)[:, : plan.own]
                    at = (own * 3 + i) * rows
                    out[to, at : at + rows, :] = block
            out[to, tail:, :] = note


def coefficients(notes):
    s00, s01, s11, c, ee, eb, ef, mixed, bc = [notes[:, i : i + 1] for i in range(9)]

    def total(value):
        return jnp.sum(value, axis=0, keepdims=True)

    norm_0 = total(s00)
    power_0 = total(s01)
    alpha_0 = norm_0 / power_0
    delta = alpha_0 - c
    norm_1 = total(ee - 2.0 * delta * eb + delta * delta * s11)
    beta = norm_1 / norm_0
    power_1 = (
        total(ef - delta * mixed + delta * delta * bc)
        + 2.0 * beta * total(eb - delta * s11)
        + beta * beta * power_0
    )
    return alpha_0, beta, norm_1 / power_1


def outputs(a, b, c, scalars):
    alpha_0, beta, alpha_1 = scalars
    residual = a - alpha_0 * b
    image = b - alpha_0 * c
    estimate = alpha_0 * a + alpha_1 * (residual + beta * a)
    return estimate, residual - alpha_1 * (image + beta * b)


def combine_kernel(plan, blocks, estimate, residual):
    rows = plan.rows
    tail = 3 * plan.own_layers * rows
    scalars = coefficients(blocks[:, tail, :])
    scalars = [jnp.broadcast_to(value, (rows, LANES)) for value in scalars]
    for k in range(plan.devices):
        for own in range(plan.own_layers):
            a, b, c = [
                blocks[k, (own * 3 + i) * rows : (own * 3 + i + 1) * rows, :] for i in range(3)
            ]
            where = pl.ds(own * rows * plan.devices + k, rows, stride=plan.devices)
            for value, ref in zip(outputs(a, b, c, scalars), (estimate, residual)):
                ref[where, :] = pltpu.roll(value, (-plan.side) % LANES, 1)


def combine(plan, blocks):
    shape = (plan.own_layers, plan.rows, plan.width)
    if plan.own == LANES:
        lines = (plan.own_layers * plan.rows * plan.devices, LANES)
        results = pl.pallas_call(
            functools.partial(combine_kernel, plan),
            out_shape=[jax.ShapeDtypeStruct(lines, jnp.float32)] * 2,
            in_specs=[pl.BlockSpec(memory_space=VMEM)],
            out_specs=[pl.BlockSpec(memory_space=VMEM)] * 2,
            name="combine",
        )(in_vmem(blocks))
        return [value.reshape(shape) for value in results]
    tail = 3 * plan.own_layers * plan.rows
    scalars = coefficients(blocks[:, tail, :])
    fields = blocks[:, :tail].reshape(plan.devices, plan.own_layers, 3, plan.rows, plan.own)
    fields = fields.transpose(2, 1, 3, 0, 4).reshape((3,) + shape)
    return outputs(*fields, [value[0, 0] for value in scalars])


def per_device(mesh, measured_slopes, valid_mask, layer_offsets, reg_weight):
    dirs, _, rows, width = measured_slopes.shape
    plan = Plan(mesh, dirs, rows, width, reg_weight.shape[0])
    column_tiles = width // LANES
    slopes = measured_slopes.reshape(dirs, 2, rows, column_tiles, LANES)
    slopes = slopes.transpose(0, 2, 3, 1, 4).reshape(dirs, rows, 2 * column_tiles, LANES)
    strips = plan.strip // LANES
    piece = (plan.sent_tiles, plan.in_rows, LANES)
    lead = () if plan.direct else (plan.tiles,)
    kind = pltpu.VMEM if plan.direct else jax.ShapeDtypeStruct
    sent = pl.pallas_call(
        functools.partial(gather_kernel, plan),
        out_shape=[kind(lead + piece, jnp.float32)] * plan.outs,
        in_specs=[pl.BlockSpec(memory_space=pl.ANY)] * 2,
        out_specs=[pl.BlockSpec(memory_space=VMEM)] * plan.outs,
        scratch_shapes=[
            pltpu.VMEM((dirs, plan.high, plan.raw_rows, LANES), jnp.float32),
            pltpu.VMEM((rows, plan.strip), jnp.int32),
            pltpu.VMEM((strips, plan.in_rows, LANES), jnp.float32),
            pltpu.VMEM((strips - 1, plan.in_rows, LANES), jnp.float32),
            pltpu.SemaphoreType.DMA((dirs, 3)),
            pltpu.SemaphoreType.DMA((3,)),
        ],
        name="gather",
    )(slopes, valid_mask)
    if plan.direct:
        fields = list(sent)
        for k in reversed(range(1, plan.outs)):
            fields[k] = lax.ppermute(sent[k], "tile", [(i, i ^ (2 * k)) for i in range(plan.tiles)])
        swap = [(i, i ^ 1) for i in range(plan.tiles)]
        fields = fields + [lax.ppermute(field, "tile", swap) for field in fields]
    else:
        fields = [lax.all_to_all(sent[0], "tile", 0, 0)]
    fields = [in_vmem(field) for field in fields]
    tall_rows = plan.grid_rows + 2 * PAD

    def scratch(*lead):
        return pltpu.VMEM(lead + (plan.lane_tiles, tall_rows, LANES), jnp.float32)

    blocks = pl.pallas_call(
        functools.partial(solve_kernel, plan),
        out_shape=kind((plan.devices, plan.out_rows, plan.own), jnp.float32),
        in_specs=[pl.BlockSpec(memory_space=SMEM)] * 2
        + [pl.BlockSpec(memory_space=VMEM)] * len(fields),
        out_specs=pl.BlockSpec(memory_space=VMEM),
        scratch_shapes=[
            scratch(dirs),
            scratch(),
            scratch(plan.layers),
            scratch(plan.layers),
            scratch(dirs, 2),
            scratch(plan.layers),
            pltpu.VMEM((3, plan.layers, plan.grid_rows, LANES), jnp.float32),
        ],
        name="solve",
    )(layer_offsets.transpose(1, 2, 0), reg_weight, *fields)
    blocks = lax.all_to_all(blocks, ("layer", "tile"), 0, 0)
    return tuple(combine(plan, blocks))


def solution(mesh):
    return jax.shard_map(
        functools.partial(per_device, mesh),
        mesh=mesh,
        in_specs=(P(None, None, "tile", None), P("tile", None), P(), P()),
        out_specs=(P("layer", "tile", None), P("layer", "tile", None)),
        check_vma=False,
    )
```

```python
import functools

import jax
import jax.numpy as jnp
from jax import lax
from jax.experimental import pallas as pl
from jax.experimental.pallas import tpu as pltpu
from jax.sharding import PartitionSpec as P

HALO = 8
LANES = 128
PAD = 8
REACH_ROW = 2 * (2 * HALO + 1)
REACH = REACH_ROW + HALO + 1
VMEM = pltpu.MemorySpace.VMEM
SMEM = pltpu.MemorySpace.SMEM


def round_up(value, unit):
    return -(-value // unit) * unit


class Plan:
    def __init__(self, mesh, dirs, rows, width, layers):
        self.layer_devices = mesh.shape["layer"]
        self.tiles = mesh.shape["tile"]
        self.devices = self.layer_devices * self.tiles
        self.dirs = dirs
        self.rows = rows
        self.width = width
        self.layers = layers
        self.own_layers = layers // self.layer_devices
        self.grid_rows = rows * self.tiles
        assert width % self.devices == 0 and layers % self.layer_devices == 0
        self.own = width // self.devices
        self.part = width // self.layer_devices
        assert self.part % LANES == 0
        self.lane_tiles = round_up(self.own + 2 * REACH, LANES) // LANES
        self.side = (self.lane_tiles * LANES - self.own) // 2
        self.margin = round_up(self.side + 1, LANES)
        self.strip = self.part + 2 * self.margin
        assert self.margin <= 4 * LANES and (2 * self.part // LANES) % 8 == 0
        self.raw_core = min(2 * self.part // LANES + 16, 2 * width // LANES)
        self.raw_rows = 2 * self.part // LANES + 32
        assert self.strip <= width
        self.high = round_up(rows + 1, 8)
        self.used_rows = dirs * (rows + 1) + rows
        self.in_rows = round_up(self.used_rows, 8)
        self.out_rows = round_up(3 * self.own_layers * rows + 1, 8)
        self.chips = self.tiles // 2
        self.direct = self.tiles in (2, 4, 8) and self.own == LANES and self.lane_tiles == 2
        self.outs = self.chips if self.direct else 1
        self.sent_tiles = self.lane_tiles + 1 if self.direct else self.lane_tiles
        self.chunk = self.grid_rows
        while self.chunk > (96 if self.direct else 192):
            self.chunk //= 2


def in_vmem(value):
    return pltpu.with_memory_space_constraint(value, VMEM)


def lane_index():
    return lax.broadcasted_iota(jnp.int32, (8, LANES), 1)


def tall(mask, rows):
    return jnp.broadcast_to(mask[:1], (rows, LANES))


def lane_shift(tiles, steps, rows):
    count = len(tiles)
    if isinstance(steps, int):
        turn = (-steps) % LANES
    else:
        turn = jnp.where(steps > 0, LANES - steps, -steps)
    turned = [pltpu.roll(tile, turn, 1) for tile in tiles]
    if count == 1:
        return turned
    source = lane_index() + steps
    past = tall(source >= LANES, rows)
    before = tall(source < 0, rows)
    if count == 2:
        outside = past | before
        return [jnp.where(outside, turned[1 - t], turned[t]) for t in range(2)]
    return [
        jnp.where(
            past,
            turned[(t + 1) % count],
            jnp.where(before, turned[(t - 1) % count], turned[t]),
        )
        for t in range(count)
    ]


def place_of():
    return lax.axis_index("layer"), lax.axis_index("tile")


def gather_kernel(plan, slopes, mask, *refs):
    outs, (raw, raw_mask, strip, ready, sems) = refs[: plan.outs], refs[plan.outs :]
    layer, tile = place_of()
    rows, dirs, part, width = plan.rows, plan.dirs, plan.part, plan.width
    side = plan.margin
    column = layer * part - side
    line = 2 * (layer * part // LANES)
    base = jnp.clip(column, 0, width - plan.strip)
    base_line = jnp.clip(line - 8, 0, 2 * width // LANES - plan.raw_core)
    slope_copies = [
        pltpu.make_async_copy(
            slopes.at[g, :, pl.ds(pl.multiple_of(base_line, 8), plan.raw_core), :],
            raw.at[g, pl.ds(0, rows), pl.ds(8, plan.raw_core), :],
            sems.at[g],
        )
        for g in range(dirs)
    ]
    mask_copy = pltpu.make_async_copy(
        mask.at[:, pl.ds(pl.multiple_of(base, LANES), plan.strip)], raw_mask, sems.at[dirs]
    )
    mask_copy.start()
    for copy in slope_copies:
        copy.start()
    mask_copy.wait()

    strips = plan.strip // LANES
    high = plan.high
    used = dirs * (rows + 1) + rows
    lane = lane_index()
    wrap = tall(lane == 0, high)
    blank = jnp.zeros((high - rows, LANES), jnp.float32)
    valid = []
    for n in range(strips):
        at = jnp.clip(column + n * LANES - base, 0, plan.strip - LANES)
        here = raw_mask[:, pl.ds(pl.multiple_of(at, LANES), LANES)].astype(jnp.float32)
        begin = column + n * LANES
        keep = jnp.where((begin >= 0) & (begin < width), here, 0.0)
        strip[n, dirs * rows : (dirs + 1) * rows, :] = keep
        if used < plan.in_rows:
            strip[n, used:, :] = jnp.zeros((plan.in_rows - used, LANES), jnp.float32)
        valid.append(keep > 0.0)
    for g in range(dirs):
        slope_copies[g].wait()
        flat = raw.at[g].reshape(high * plan.raw_rows, LANES)
        before = None
        for n in range(strips):
            at = line - base_line + 2 * n + 8 - 2 * (side // LANES)
            slope_x = flat[pl.ds(at, rows, stride=plan.raw_rows), :]
            slope_y = flat[pl.ds(at + 1, rows, stride=plan.raw_rows), :]
            both = jnp.concatenate([jnp.where(valid[n], slope_x + slope_y, 0.0), blank], axis=0)
            diff = jnp.concatenate([jnp.where(valid[n], slope_x - slope_y, 0.0), blank], axis=0)
            c = pltpu.roll(diff + pltpu.roll(both, 1, 0), 1, 1)
            shifted = c if before is None else jnp.where(wrap, before, c)
            before = c
            field = shifted - (both + pltpu.roll(diff, 1, 0))
            if n >= strips - side // LANES:
                inside = column + n * LANES + lane < width
                field = jnp.where(tall(inside, high), field, 0.0)
            strip[n, g * rows : (g + 1) * rows, :] = field[:rows]
            carry = (dirs + 1) * rows + g
            strip[n, carry : carry + 1, :] = field[rows : rows + 1]
    turned = {}

    def turn(n, by):
        if by == 0:
            return strip[n]
        for at in (n, n + 1):
            if (at, by) not in turned:
                turned[at, by] = pltpu.roll(strip[at], (-by) % LANES, 1)
        near = tall(lane < LANES - by, plan.in_rows)
        return jnp.where(near, turned[n, by], turned[n + 1, by])

    begin = plan.margin - plan.side
    if plan.direct:
        for n in range(2 * plan.chips + 1):
            ready[n] = turn(begin // LANES + n, begin % LANES)
        for k, out in enumerate(outs):
            at = 2 * ((tile // 2) ^ k)
            for n in range(plan.sent_tiles):
                out[plan.used_rows * n : plan.used_rows * (n + 1), :] = ready[
                    at + n, : plan.used_rows, :
                ]
        return
    for t in range(plan.tiles):
        at = begin + t * plan.own
        for n in range(plan.lane_tiles):
            outs[0][t, n] = turn(at // LANES + n, at % LANES)


def solve_kernel(plan, offsets, weights, *refs):
    count = 2 * plan.outs if plan.direct else 1
    fields, (out, q, keep, v0, v1, phase, smooth, packed) = refs[:count], refs[count:]
    layers, dirs, rows = plan.layers, plan.dirs, plan.rows
    total, tiles = plan.grid_rows, range(plan.lane_tiles)
    chunk = plan.chunk
    starts = range(0, total, chunk)
    unrolled = plan.direct
    layer_place, tile_place = place_of()
    first = (layer_place * plan.tiles + tile_place) * plan.own - plan.side
    lane = lane_index()
    in_grid = []
    owned = []
    for t in tiles:
        local = lane + t * LANES
        column = local + first
        in_grid.append(tall(jnp.where((column >= 0) & (column < plan.width), 1.0, 0.0), chunk))
        owned.append(tall((local >= plan.side) & (local < plan.side + plan.own), chunk))
    two = plan.lane_tiles == 2 and plan.own == LANES

    def pack(window):
        if two:
            return jnp.where(owned[1], window[1], window[0])
        value = jnp.where(owned[0], window[0], 0.0)
        for t in tiles[1:]:
            value = jnp.where(owned[t], window[t], value)
        return value

    def packed_shift(window, steps):
        if not two:
            return pack(lane_shift(window, steps, chunk))
        turn = (-steps) % LANES if isinstance(steps, int) else jnp.where(steps > 0, LANES - steps, -steps)
        low = tall(lane < plan.side + steps, chunk)
        return pltpu.roll(jnp.where(low, window[1], window[0]), turn, 1)

    edge = jnp.zeros((PAD, LANES), jnp.float32)
    above, below = slice(0, PAD), slice(PAD + total, PAD + total + PAD)
    for t in tiles:
        keep[t, above, :] = edge
        keep[t, below, :] = edge
        for g in range(dirs):
            q[g, t, above, :] = edge
            q[g, t, below, :] = edge
            for i in range(2):
                phase[g, i, t, above, :] = edge
                phase[g, i, t, below, :] = edge
        for layer in range(layers):
            for ref in (v0, v1, smooth):
                ref[layer, t, above, :] = edge
                ref[layer, t, below, :] = edge
    sources = []
    if plan.direct:
        core = tile_place % 2
        for i, field in enumerate(fields):
            tile = 2 * ((tile_place // 2) ^ (i % plan.outs)) + (core if i < plan.outs else 1 - core)
            low = [(core + t) * plan.used_rows for t in tiles]
            sources.append((tile, [(field, start) for start in low]))
    else:
        for tile in range(plan.tiles):
            sources.append((tile, [(fields[0].at[tile, t], 0) for t in tiles]))
    for tile, windows in sources:
        here = pl.ds(PAD + tile * rows, rows)
        for t, (window, start) in enumerate(windows):
            keep[t, here, :] = window[pl.ds(start + dirs * rows, rows), :]
            for g in range(dirs):
                q[g, t, here, :] = window[pl.ds(start + g * rows, rows), :]
    for tile, windows in sources:
        below = pl.ds(PAD + (tile + 1) * rows, 1)
        counts = jnp.where(tile + 1 < plan.tiles, 1.0, 0.0)
        for t, (window, start) in enumerate(windows):
            for g in range(dirs):
                carry = start + (dirs + 1) * rows + g
                q[g, t, below, :] += window[pl.ds(carry, 1), :] * counts

    def four(x, up, down, left, right):
        return 4.0 * x - (up + down) - (left + right)

    def rows_at(r, by=0):
        return slice(PAD + r + by, PAD + r + by + chunk)

    def staged(first, second):
        for i, r in enumerate(starts):
            first(r)
            if i:
                second(starts[i - 1])
        second(starts[-1])

    def laplace(ref, layer, r, shift):
        x = [ref[layer, t, rows_at(r), :] for t in tiles]
        right = shift(x, 1)
        left = shift(x, -1)
        column = [
            4.0 * x[t] - (ref[layer, t, rows_at(r, -1), :] + ref[layer, t, rows_at(r, 1), :])
            for t in tiles
        ]
        if shift is packed_shift:
            return [pack(column) - (left + right)]
        return [column[t] - (left[t] + right[t]) for t in tiles]

    def window_shift(window, steps):
        return lane_shift(window, steps, chunk)

    def back_project(layer, level):
        source = (None, v0, v1)[level]
        shift = packed_shift if level == 2 else window_shift

        def smoothing(r):
            if source is not None:
                for t, value in enumerate(laplace(source, layer, r, window_shift)):
                    smooth[layer, t, rows_at(r), :] = value * in_grid[t]

        def adding(r):
            sums = None
            for g in range(dirs):
                low = PAD + r - offsets[layer, 0, g]
                window = [q[g, t, pl.ds(low, chunk), :] for t in tiles]
                moved = shift(window, -offsets[layer, 1, g])
                moved = [moved] if level == 2 else moved
                sums = moved if sums is None else [s + m for s, m in zip(sums, moved)]
            sums = [0.5 * value for value in sums]
            if source is not None:
                weight = weights[layer]
                sums = [s + weight * value for s, value in zip(sums, laplace(smooth, layer, r, shift))]
            if level == 2:
                packed[2, layer, r : r + chunk, :] = sums[0]
                return
            sums = [s * inside for s, inside in zip(sums, in_grid)]
            for t in tiles:
                (v0, v1)[level][layer, t, rows_at(r), :] = sums[t]
            packed[level, layer, r : r + chunk, :] = pack(sums)

        staged(smoothing, adding)

    def project(g, source):
        def phases(r):
            sums = None
            for layer in range(layers):
                low = PAD + r + offsets[layer, 0, g]
                window = [source[layer, t, pl.ds(low, chunk), :] for t in tiles]
                moved = lane_shift(window, offsets[layer, 1, g], chunk)
                sums = moved if sums is None else [s + m for s, m in zip(sums, moved)]
            sums = [s * inside for s, inside in zip(sums, in_grid)]
            right = lane_shift(sums, 1, chunk)
            for t in tiles:
                phase[g, 0, t, rows_at(r), :] = sums[t]
                phase[g, 1, t, rows_at(r), :] = right[t]

        def slopes(r):
            ahead, level = [], []
            for t in tiles:
                p00, p01 = phase[g, 0, t, rows_at(r), :], phase[g, 1, t, rows_at(r), :]
                p10, p11 = phase[g, 0, t, rows_at(r, 1), :], phase[g, 1, t, rows_at(r, 1), :]
                up0, up1 = phase[g, 0, t, rows_at(r, -1), :], phase[g, 1, t, rows_at(r, -1), :]
                mask, mask_up = keep[t, rows_at(r), :], keep[t, rows_at(r, -1), :]
                ahead.append(mask * (p01 - p10) + mask_up * (p01 - up0))
                level.append(mask * (p11 - p00) + mask_up * (up1 - p00))
            ahead = lane_shift(ahead, -1, chunk)
            for t in tiles:
                q[g, t, rows_at(r), :] = (ahead[t] - level[t]) * in_grid[t]

        staged(phases, slopes)

    def each(count, body):
        if unrolled:
            for i in range(count):
                body(i)
            return

        def step(i, carry):
            body(i)
            return carry

        lax.fori_loop(0, count, step, 0)

    def fold(value):
        return jnp.sum(value.reshape(chunk // 8, 8, LANES), axis=0)

    def inner(terms, layer, sums):
        for r in starts:
            values = terms([packed[i, layer, r : r + chunk, :] for i in range(3)])
            sums = [s + fold(value) for s, value in zip(sums, values)]
        return sums

    def send(i, layer):
        device, own = layer // plan.own_layers, layer % plan.own_layers
        for s in range(plan.tiles):
            block = packed[i, layer, s * rows : (s + 1) * rows, :]
            if plan.own < LANES:
                block = pltpu.roll(block, (-plan.side) % LANES, 1)[:, : plan.own]
            at = (own * 3 + i) * rows
            out[device * plan.tiles + s, at : at + rows, :] = block

    def first_terms(fields):
        a, b, _ = fields
        return a * a, a * b, b * b

    each(layers, lambda layer: back_project(layer, 0))
    each(dirs, lambda g: project(g, v0))
    each(layers, lambda layer: back_project(layer, 1))
    def second_terms(fields):
        a, b, c = fields
        e = a - spread * b
        f = b - spread * c
        return e * e, e * b, e * f, e * c + b * f, b * c

    sums = [jnp.zeros((8, LANES), jnp.float32)] * 3
    more = [jnp.zeros((8, LANES), jnp.float32)] * 5
    if not unrolled:
        each(dirs, lambda g: project(g, v1))
    for i in range(max(layers, dirs)):
        if unrolled and i < dirs:
            project(i, v1)
        if i < layers:
            sums = inner(first_terms, i, sums)
            send(0, i)
            send(1, i)
    s00, s01, s11 = [jnp.sum(value, keepdims=True) for value in sums]
    coefficient = jnp.where(s11 > 0.0, s01 / jnp.where(s11 > 0.0, s11, 1.0), 0.0)
    spread = jnp.broadcast_to(coefficient, (chunk, LANES))
    if not unrolled:
        each(layers, lambda layer: back_project(layer, 2))
    for layer in range(layers):
        if unrolled:
            back_project(layer, 2)
        more = inner(second_terms, layer, more)
        send(2, layer)
    more = [jnp.sum(value, keepdims=True) for value in more]
    scalars = [s00, s01, s11, coefficient] + more
    row = jnp.zeros((1, LANES), jnp.float32)
    for i, value in enumerate(scalars):
        row = jnp.where(lane[:1] == i, value, row)
    tail = 3 * plan.own_layers * rows
    note = jnp.broadcast_to(row[:, : plan.own], (plan.out_rows - tail, plan.own))
    for to in range(plan.devices):
        out[to, tail:, :] = note


def coefficients(notes):
    s00, s01, s11, c, ee, eb, ef, mixed, bc = [notes[:, i : i + 1] for i in range(9)]

    def total(value):
        return jnp.sum(value, axis=0, keepdims=True)

    norm_0 = total(s00)
    power_0 = total(s01)
    alpha_0 = norm_0 / power_0
    delta = alpha_0 - c
    norm_1 = total(ee - 2.0 * delta * eb + delta * delta * s11)
    beta = norm_1 / norm_0
    power_1 = (
        total(ef - delta * mixed + delta * delta * bc)
        + 2.0 * beta * total(eb - delta * s11)
        + beta * beta * power_0
    )
    return alpha_0, beta, norm_1 / power_1


def weights_of(scalars):
    alpha_0, beta, alpha_1 = scalars
    return alpha_0 + alpha_1 * (1.0 + beta), -alpha_1 * alpha_0


def combine_kernel(plan, blocks, estimate, residual, lines, sems):
    rows = plan.rows
    tail = 3 * plan.own_layers * rows
    near, far = [
        jnp.broadcast_to(value, (rows, LANES))
        for value in weights_of(coefficients(blocks[:, tail, :]))
    ]
    copies = [
        pltpu.make_async_copy(lines.at[i], ref, sems.at[i])
        for i, ref in enumerate((estimate, residual))
    ]
    for i, copy in enumerate(copies):
        for k in range(plan.devices):
            for own in range(plan.own_layers):
                field = [
                    blocks[k, (own * 3 + j) * rows : (own * 3 + j + 1) * rows, :]
                    for j in range(i, i + 2)
                ]
                value = near * field[0] + far * field[1]
                if i:
                    value = blocks[k, own * 3 * rows : (own * 3 + 1) * rows, :] - value
                where = pl.ds(own * rows * plan.devices + k, rows, stride=plan.devices)
                lines.at[i][where, :] = pltpu.roll(value, (-plan.side) % LANES, 1)
        copy.start()
    for copy in copies:
        copy.wait()


def combine(plan, blocks):
    shape = (plan.own_layers, plan.rows, plan.width)
    if plan.own == LANES:
        lines = (plan.own_layers * plan.rows * plan.devices, LANES)
        results = pl.pallas_call(
            functools.partial(combine_kernel, plan),
            out_shape=[jax.ShapeDtypeStruct(lines, jnp.float32)] * 2,
            in_specs=[pl.BlockSpec(memory_space=VMEM)],
            out_specs=[pl.BlockSpec(memory_space=pl.ANY)] * 2,
            scratch_shapes=[
                pltpu.VMEM((2,) + lines, jnp.float32),
                pltpu.SemaphoreType.DMA((2,)),
            ],
            name="combine",
        )(in_vmem(blocks))
        return [value.reshape(shape) for value in results]
    tail = 3 * plan.own_layers * plan.rows
    scalars = coefficients(blocks[:, tail, :])
    fields = blocks[:, :tail].reshape(plan.devices, plan.own_layers, 3, plan.rows, plan.own)
    fields = fields.transpose(2, 1, 3, 0, 4).reshape((3,) + shape)
    near, far = weights_of([value[0, 0] for value in scalars])
    a, b, c = fields
    return near * a + far * b, a - (near * b + far * c)


def per_device(mesh, measured_slopes, valid_mask, layer_offsets, reg_weight):
    dirs, _, rows, width = measured_slopes.shape
    plan = Plan(mesh, dirs, rows, width, reg_weight.shape[0])
    column_tiles = width // LANES
    slopes = measured_slopes.reshape(dirs, 2, rows, column_tiles, LANES)
    slopes = slopes.transpose(0, 2, 3, 1, 4).reshape(dirs, rows, 2 * column_tiles, LANES)
    strips = plan.strip // LANES
    piece = (plan.tiles, plan.sent_tiles, plan.in_rows, LANES)
    if plan.direct:
        piece = (round_up(plan.sent_tiles * plan.used_rows, 8), LANES)
    kind = pltpu.VMEM if plan.direct else jax.ShapeDtypeStruct
    sent = pl.pallas_call(
        functools.partial(gather_kernel, plan),
        out_shape=[kind(piece, jnp.float32)] * plan.outs,
        in_specs=[pl.BlockSpec(memory_space=pl.ANY)] * 2,
        out_specs=[pl.BlockSpec(memory_space=VMEM)] * plan.outs,
        scratch_shapes=[
            pltpu.VMEM((dirs, plan.high, plan.raw_rows, LANES), jnp.float32),
            pltpu.VMEM((rows, plan.strip), jnp.int32),
            pltpu.VMEM((strips, plan.in_rows, LANES), jnp.float32),
            pltpu.VMEM((strips - 1, plan.in_rows, LANES), jnp.float32),
            pltpu.SemaphoreType.DMA((dirs + 1,)),
        ],
        name="gather",
    )(slopes, valid_mask)
    if plan.direct:
        fields = list(sent)
        for k in reversed(range(1, plan.outs)):
            fields[k] = lax.ppermute(sent[k], "tile", [(i, i ^ (2 * k)) for i in range(plan.tiles)])
        swap = [(i, i ^ 1) for i in range(plan.tiles)]
        fields = fields + [lax.ppermute(field, "tile", swap) for field in fields]
    else:
        fields = [lax.all_to_all(sent[0], "tile", 0, 0)]
    fields = [in_vmem(field) for field in fields]
    tall_rows = plan.grid_rows + 2 * PAD

    def scratch(*lead):
        return pltpu.VMEM(lead + (plan.lane_tiles, tall_rows, LANES), jnp.float32)

    blocks = pl.pallas_call(
        functools.partial(solve_kernel, plan),
        out_shape=kind((plan.devices, plan.out_rows, plan.own), jnp.float32),
        in_specs=[pl.BlockSpec(memory_space=SMEM)] * 2
        + [pl.BlockSpec(memory_space=VMEM)] * len(fields),
        out_specs=pl.BlockSpec(memory_space=VMEM),
        scratch_shapes=[
            scratch(dirs),
            scratch(),
            scratch(plan.layers),
            scratch(plan.layers),
            scratch(dirs, 2),
            scratch(plan.layers),
            pltpu.VMEM((3, plan.layers, plan.grid_rows, LANES), jnp.float32),
        ],
        name="solve",
    )(layer_offsets.transpose(1, 2, 0), reg_weight, *fields)
    blocks = lax.all_to_all(blocks, ("layer", "tile"), 0, 0)
    return tuple(combine(plan, blocks))


def solution(mesh):
    return jax.shard_map(
        functools.partial(per_device, mesh),
        mesh=mesh,
        in_specs=(P(None, None, "tile", None), P("tile", None), P(), P()),
        out_specs=(P("layer", "tile", None), P("layer", "tile", None)),
        check_vma=False,
    )
```

```python
import functools

import jax
import jax.numpy as jnp
from jax import lax
from jax.experimental import pallas as pl
from jax.experimental.pallas import tpu as pltpu
from jax.sharding import PartitionSpec as P

HALO = 8
LANES = 128
PAD = 8
REACH_ROW = 2 * (2 * HALO + 1)
REACH = REACH_ROW + HALO + 1
VMEM = pltpu.MemorySpace.VMEM
SMEM = pltpu.MemorySpace.SMEM


def round_up(value, unit):
    return -(-value // unit) * unit


class Plan:
    def __init__(self, mesh, dirs, rows, width, layers):
        self.layer_devices = mesh.shape["layer"]
        self.tiles = mesh.shape["tile"]
        self.devices = self.layer_devices * self.tiles
        self.dirs = dirs
        self.rows = rows
        self.width = width
        self.layers = layers
        self.own_layers = layers // self.layer_devices
        self.grid_rows = rows * self.tiles
        assert width % self.devices == 0 and layers % self.layer_devices == 0
        self.own = width // self.devices
        self.part = width // self.layer_devices
        assert self.part % LANES == 0
        self.lane_tiles = round_up(self.own + 2 * REACH, LANES) // LANES
        self.side = (self.lane_tiles * LANES - self.own) // 2
        self.margin = round_up(self.side + 1, LANES)
        self.high = round_up(rows + 1, 8)
        self.used_rows = dirs * (rows + 1) + rows
        self.in_rows = round_up(self.used_rows, 8)
        self.out_rows = round_up(3 * self.own_layers * rows + 1, 8)
        self.chips = self.tiles // 2
        self.direct = self.tiles in (2, 4, 8) and self.own == LANES and self.lane_tiles == 2
        self.outs = self.chips if self.direct else 1
        self.halves = 1
        if self.direct and self.chips == 4 and self.part % (8 * LANES) == 0:
            self.halves = 2
        self.stretch = self.part // self.halves
        self.strip = self.stretch + 2 * self.margin
        assert self.margin <= 4 * LANES and (2 * self.stretch // LANES) % 8 == 0
        self.raw_core = min(2 * self.stretch // LANES + 16, 2 * width // LANES)
        self.raw_rows = 2 * self.stretch // LANES + 32
        assert self.strip <= width
        self.sent_tiles = self.lane_tiles + 1 if self.direct else self.lane_tiles
        self.chunk = self.grid_rows
        while self.chunk > (96 if self.direct else 192):
            self.chunk //= 2


def in_vmem(value):
    return pltpu.with_memory_space_constraint(value, VMEM)


def lane_index():
    return lax.broadcasted_iota(jnp.int32, (8, LANES), 1)


def tall(mask, rows):
    return jnp.broadcast_to(mask[:1], (rows, LANES))


def lane_shift(tiles, steps, rows):
    count = len(tiles)
    if isinstance(steps, int):
        turn = (-steps) % LANES
    else:
        turn = jnp.where(steps > 0, LANES - steps, -steps)
    turned = [pltpu.roll(tile, turn, 1) for tile in tiles]
    if count == 1:
        return turned
    source = lane_index() + steps
    past = tall(source >= LANES, rows)
    before = tall(source < 0, rows)
    if count == 2:
        outside = past | before
        return [jnp.where(outside, turned[1 - t], turned[t]) for t in range(2)]
    return [
        jnp.where(
            past,
            turned[(t + 1) % count],
            jnp.where(before, turned[(t - 1) % count], turned[t]),
        )
        for t in range(count)
    ]


def place_of():
    return lax.axis_index("layer"), lax.axis_index("tile")


def gather_kernel(plan, slots, slopes, mask, *refs):
    count = len(slots) if plan.direct else 1
    outs, (raw, raw_mask, strip, ready, sems) = refs[-5 - count : -5], refs[-5:]
    layer, tile = place_of()
    rows, dirs, width = plan.rows, plan.dirs, plan.width
    side = plan.margin
    stretch = layer * plan.halves
    if plan.halves == 2:
        stretch = stretch + (((tile // 2) ^ slots[0]) // 2)
    column = stretch * plan.stretch - side
    line = stretch * (2 * plan.stretch // LANES)
    base = jnp.clip(column, 0, width - plan.strip)
    base_line = jnp.clip(line - 8, 0, 2 * width // LANES - plan.raw_core)
    slope_copies = [
        pltpu.make_async_copy(
            slopes.at[g, :, pl.ds(pl.multiple_of(base_line, 8), plan.raw_core), :],
            raw.at[g, pl.ds(0, rows), pl.ds(8, plan.raw_core), :],
            sems.at[g],
        )
        for g in range(dirs)
    ]
    mask_copy = pltpu.make_async_copy(
        mask.at[:, pl.ds(pl.multiple_of(base, LANES), plan.strip)], raw_mask, sems.at[dirs]
    )
    mask_copy.start()
    for copy in slope_copies:
        copy.start()
    mask_copy.wait()

    strips = plan.strip // LANES
    high = plan.high
    used = dirs * (rows + 1) + rows
    lane = lane_index()
    wrap = tall(lane == 0, high)
    blank = jnp.zeros((high - rows, LANES), jnp.float32)
    valid = []
    for n in range(strips):
        at = jnp.clip(column + n * LANES - base, 0, plan.strip - LANES)
        here = raw_mask[:, pl.ds(pl.multiple_of(at, LANES), LANES)].astype(jnp.float32)
        begin = column + n * LANES
        keep = jnp.where((begin >= 0) & (begin < width), here, 0.0)
        strip[n, dirs * rows : (dirs + 1) * rows, :] = keep
        if used < plan.in_rows:
            strip[n, used:, :] = jnp.zeros((plan.in_rows - used, LANES), jnp.float32)
        valid.append(keep > 0.0)
    for g in range(dirs):
        slope_copies[g].wait()
        flat = raw.at[g].reshape(high * plan.raw_rows, LANES)
        before = None
        for n in range(strips):
            at = line - base_line + 2 * n + 8 - 2 * (side // LANES)
            slope_x = flat[pl.ds(at, rows, stride=plan.raw_rows), :]
            slope_y = flat[pl.ds(at + 1, rows, stride=plan.raw_rows), :]
            both = jnp.concatenate([jnp.where(valid[n], slope_x + slope_y, 0.0), blank], axis=0)
            diff = jnp.concatenate([jnp.where(valid[n], slope_x - slope_y, 0.0), blank], axis=0)
            c = pltpu.roll(diff + pltpu.roll(both, 1, 0), 1, 1)
            shifted = c if before is None else jnp.where(wrap, before, c)
            before = c
            field = shifted - (both + pltpu.roll(diff, 1, 0))
            if n >= strips - side // LANES:
                inside = column + n * LANES + lane < width
                field = jnp.where(tall(inside, high), field, 0.0)
            strip[n, g * rows : (g + 1) * rows, :] = field[:rows]
            carry = (dirs + 1) * rows + g
            strip[n, carry : carry + 1, :] = field[rows : rows + 1]
    turned = {}

    def turn(n, by):
        if by == 0:
            return strip[n]
        for at in (n, n + 1):
            if (at, by) not in turned:
                turned[at, by] = pltpu.roll(strip[at], (-by) % LANES, 1)
        near = tall(lane < LANES - by, plan.in_rows)
        return jnp.where(near, turned[n, by], turned[n + 1, by])

    begin = plan.margin - plan.side
    if plan.direct:
        near = plan.chips // plan.halves
        for n in range(2 * near + 1):
            ready[n] = turn(begin // LANES + n, begin % LANES)
        for k, out in zip(slots, outs):
            at = 2 * (((tile // 2) ^ k) % near)
            for n in range(plan.sent_tiles):
                out[plan.used_rows * n : plan.used_rows * (n + 1), :] = ready[
                    at + n, : plan.used_rows, :
                ]
        return
    for t in range(plan.tiles):
        at = begin + t * plan.own
        for n in range(plan.lane_tiles):
            outs[0][t, n] = turn(at // LANES + n, at % LANES)


def solve_kernel(plan, offsets, weights, *refs):
    count = 2 * plan.outs if plan.direct else 1
    fields, (out, q, keep, v0, v1, phase, smooth, packed) = refs[:count], refs[count:]
    layers, dirs, rows = plan.layers, plan.dirs, plan.rows
    total, tiles = plan.grid_rows, range(plan.lane_tiles)
    chunk = plan.chunk
    starts = range(0, total, chunk)
    unrolled = plan.direct
    layer_place, tile_place = place_of()
    first = (layer_place * plan.tiles + tile_place) * plan.own - plan.side
    lane = lane_index()
    in_grid = []
    owned = []
    for t in tiles:
        local = lane + t * LANES
        column = local + first
        in_grid.append(tall(jnp.where((column >= 0) & (column < plan.width), 1.0, 0.0), chunk))
        owned.append(tall((local >= plan.side) & (local < plan.side + plan.own), chunk))
    two = plan.lane_tiles == 2 and plan.own == LANES

    def pack(window):
        if two:
            return jnp.where(owned[1], window[1], window[0])
        value = jnp.where(owned[0], window[0], 0.0)
        for t in tiles[1:]:
            value = jnp.where(owned[t], window[t], value)
        return value

    def packed_shift(window, steps):
        if not two:
            return pack(lane_shift(window, steps, chunk))
        turn = (-steps) % LANES if isinstance(steps, int) else jnp.where(steps > 0, LANES - steps, -steps)
        low = tall(lane < plan.side + steps, chunk)
        return pltpu.roll(jnp.where(low, window[1], window[0]), turn, 1)

    edge = jnp.zeros((PAD, LANES), jnp.float32)
    above, below = slice(0, PAD), slice(PAD + total, PAD + total + PAD)
    for t in tiles:
        keep[t, above, :] = edge
        keep[t, below, :] = edge
        for g in range(dirs):
            q[g, t, above, :] = edge
            q[g, t, below, :] = edge
            for i in range(2):
                phase[g, i, t, above, :] = edge
                phase[g, i, t, below, :] = edge
        for layer in range(layers):
            for ref in (v0, v1, smooth):
                ref[layer, t, above, :] = edge
                ref[layer, t, below, :] = edge
    sources = []
    if plan.direct:
        core = tile_place % 2
        for i, field in enumerate(fields):
            tile = 2 * ((tile_place // 2) ^ (i % plan.outs)) + (core if i < plan.outs else 1 - core)
            low = [(core + t) * plan.used_rows for t in tiles]
            sources.append((tile, [(field, start) for start in low]))
    else:
        for tile in range(plan.tiles):
            sources.append((tile, [(fields[0].at[tile, t], 0) for t in tiles]))
    for tile, windows in sources:
        here = pl.ds(PAD + tile * rows, rows)
        for t, (window, start) in enumerate(windows):
            keep[t, here, :] = window[pl.ds(start + dirs * rows, rows), :]
            for g in range(dirs):
                q[g, t, here, :] = window[pl.ds(start + g * rows, rows), :]
    for tile, windows in sources:
        below = pl.ds(PAD + (tile + 1) * rows, 1)
        counts = jnp.where(tile + 1 < plan.tiles, 1.0, 0.0)
        for t, (window, start) in enumerate(windows):
            for g in range(dirs):
                carry = start + (dirs + 1) * rows + g
                q[g, t, below, :] += window[pl.ds(carry, 1), :] * counts

    def four(x, up, down, left, right):
        return 4.0 * x - (up + down) - (left + right)

    def rows_at(r, by=0):
        return slice(PAD + r + by, PAD + r + by + chunk)

    def staged(first, second):
        for i, r in enumerate(starts):
            first(r)
            if i:
                second(starts[i - 1])
        second(starts[-1])

    def laplace(ref, layer, r, shift):
        x = [ref[layer, t, rows_at(r), :] for t in tiles]
        right = shift(x, 1)
        left = shift(x, -1)
        column = [
            4.0 * x[t] - (ref[layer, t, rows_at(r, -1), :] + ref[layer, t, rows_at(r, 1), :])
            for t in tiles
        ]
        if shift is packed_shift:
            return [pack(column) - (left + right)]
        return [column[t] - (left[t] + right[t]) for t in tiles]

    def window_shift(window, steps):
        return lane_shift(window, steps, chunk)

    def back_project(layer, level):
        source = (None, v0, v1)[level]
        shift = packed_shift if level == 2 else window_shift

        def smoothing(r):
            if source is not None:
                for t, value in enumerate(laplace(source, layer, r, window_shift)):
                    smooth[layer, t, rows_at(r), :] = value * in_grid[t]

        def adding(r):
            sums = None
            for g in range(dirs):
                low = PAD + r - offsets[layer, 0, g]
                window = [q[g, t, pl.ds(low, chunk), :] for t in tiles]
                moved = shift(window, -offsets[layer, 1, g])
                moved = [moved] if level == 2 else moved
                sums = moved if sums is None else [s + m for s, m in zip(sums, moved)]
            sums = [0.5 * value for value in sums]
            if source is not None:
                weight = weights[layer]
                sums = [s + weight * value for s, value in zip(sums, laplace(smooth, layer, r, shift))]
            if level == 2:
                packed[2, layer, r : r + chunk, :] = sums[0]
                return
            sums = [s * inside for s, inside in zip(sums, in_grid)]
            for t in tiles:
                (v0, v1)[level][layer, t, rows_at(r), :] = sums[t]
            packed[level, layer, r : r + chunk, :] = pack(sums)

        staged(smoothing, adding)

    def project(g, source):
        def phases(r):
            sums = None
            for layer in range(layers):
                low = PAD + r + offsets[layer, 0, g]
                window = [source[layer, t, pl.ds(low, chunk), :] for t in tiles]
                moved = lane_shift(window, offsets[layer, 1, g], chunk)
                sums = moved if sums is None else [s + m for s, m in zip(sums, moved)]
            sums = [s * inside for s, inside in zip(sums, in_grid)]
            right = lane_shift(sums, 1, chunk)
            for t in tiles:
                phase[g, 0, t, rows_at(r), :] = sums[t]
                phase[g, 1, t, rows_at(r), :] = right[t]

        def slopes(r):
            ahead, level = [], []
            for t in tiles:
                p00, p01 = phase[g, 0, t, rows_at(r), :], phase[g, 1, t, rows_at(r), :]
                p10, p11 = phase[g, 0, t, rows_at(r, 1), :], phase[g, 1, t, rows_at(r, 1), :]
                up0, up1 = phase[g, 0, t, rows_at(r, -1), :], phase[g, 1, t, rows_at(r, -1), :]
                mask, mask_up = keep[t, rows_at(r), :], keep[t, rows_at(r, -1), :]
                ahead.append(mask * (p01 - p10) + mask_up * (p01 - up0))
                level.append(mask * (p11 - p00) + mask_up * (up1 - p00))
            ahead = lane_shift(ahead, -1, chunk)
            for t in tiles:
                q[g, t, rows_at(r), :] = (ahead[t] - level[t]) * in_grid[t]

        staged(phases, slopes)

    def each(count, body):
        if unrolled:
            for i in range(count):
                body(i)
            return

        def step(i, carry):
            body(i)
            return carry

        lax.fori_loop(0, count, step, 0)

    def fold(value):
        return jnp.sum(value.reshape(chunk // 8, 8, LANES), axis=0)

    def inner(terms, layer, sums):
        for r in starts:
            values = terms([packed[i, layer, r : r + chunk, :] for i in range(3)])
            sums = [s + fold(value) for s, value in zip(sums, values)]
        return sums

    def send(i, layer):
        device, own = layer // plan.own_layers, layer % plan.own_layers
        for s in range(plan.tiles):
            block = packed[i, layer, s * rows : (s + 1) * rows, :]
            if plan.own < LANES:
                block = pltpu.roll(block, (-plan.side) % LANES, 1)[:, : plan.own]
            at = (own * 3 + i) * rows
            out[device * plan.tiles + s, at : at + rows, :] = block

    def first_terms(fields):
        a, b, _ = fields
        return a * a, a * b, b * b

    each(layers, lambda layer: back_project(layer, 0))
    each(dirs, lambda g: project(g, v0))
    each(layers, lambda layer: back_project(layer, 1))
    def second_terms(fields):
        a, b, c = fields
        e = a - spread * b
        f = b - spread * c
        return e * e, e * b, e * f, e * c + b * f, b * c

    sums = [jnp.zeros((8, LANES), jnp.float32)] * 3
    more = [jnp.zeros((8, LANES), jnp.float32)] * 5
    if not unrolled:
        each(dirs, lambda g: project(g, v1))
    for i in range(max(layers, dirs)):
        if unrolled and i < dirs:
            project(i, v1)
        if i < layers:
            sums = inner(first_terms, i, sums)
            send(0, i)
            send(1, i)
    s00, s01, s11 = [jnp.sum(value, keepdims=True) for value in sums]
    coefficient = jnp.where(s11 > 0.0, s01 / jnp.where(s11 > 0.0, s11, 1.0), 0.0)
    spread = jnp.broadcast_to(coefficient, (chunk, LANES))
    if not unrolled:
        each(layers, lambda layer: back_project(layer, 2))
    for layer in range(layers):
        if unrolled:
            back_project(layer, 2)
        more = inner(second_terms, layer, more)
        send(2, layer)
    more = [jnp.sum(value, keepdims=True) for value in more]
    scalars = [s00, s01, s11, coefficient] + more
    row = jnp.zeros((1, LANES), jnp.float32)
    for i, value in enumerate(scalars):
        row = jnp.where(lane[:1] == i, value, row)
    tail = 3 * plan.own_layers * rows
    note = jnp.broadcast_to(row[:, : plan.own], (plan.out_rows - tail, plan.own))
    for to in range(plan.devices):
        out[to, tail:, :] = note


def coefficients(notes):
    s00, s01, s11, c, ee, eb, ef, mixed, bc = [notes[:, i : i + 1] for i in range(9)]

    def total(value):
        return jnp.sum(value, axis=0, keepdims=True)

    norm_0 = total(s00)
    power_0 = total(s01)
    alpha_0 = norm_0 / power_0
    delta = alpha_0 - c
    norm_1 = total(ee - 2.0 * delta * eb + delta * delta * s11)
    beta = norm_1 / norm_0
    power_1 = (
        total(ef - delta * mixed + delta * delta * bc)
        + 2.0 * beta * total(eb - delta * s11)
        + beta * beta * power_0
    )
    return alpha_0, beta, norm_1 / power_1


def weights_of(scalars):
    alpha_0, beta, alpha_1 = scalars
    return alpha_0 + alpha_1 * (1.0 + beta), -alpha_1 * alpha_0


def combine_kernel(plan, blocks, estimate, residual, lines, sems):
    rows = plan.rows
    tail = 3 * plan.own_layers * rows
    near, far = [
        jnp.broadcast_to(value, (rows, LANES))
        for value in weights_of(coefficients(blocks[:, tail, :]))
    ]
    copies = [
        pltpu.make_async_copy(lines.at[i], ref, sems.at[i])
        for i, ref in enumerate((estimate, residual))
    ]
    for i, copy in enumerate(copies):
        for k in range(plan.devices):
            for own in range(plan.own_layers):
                field = [
                    blocks[k, (own * 3 + j) * rows : (own * 3 + j + 1) * rows, :]
                    for j in range(i, i + 2)
                ]
                value = near * field[0] + far * field[1]
                if i:
                    value = blocks[k, own * 3 * rows : (own * 3 + 1) * rows, :] - value
                where = pl.ds(own * rows * plan.devices + k, rows, stride=plan.devices)
                lines.at[i][where, :] = pltpu.roll(value, (-plan.side) % LANES, 1)
        copy.start()
    for copy in copies:
        copy.wait()


def combine(plan, blocks):
    shape = (plan.own_layers, plan.rows, plan.width)
    if plan.own == LANES:
        lines = (plan.own_layers * plan.rows * plan.devices, LANES)
        results = pl.pallas_call(
            functools.partial(combine_kernel, plan),
            out_shape=[jax.ShapeDtypeStruct(lines, jnp.float32)] * 2,
            in_specs=[pl.BlockSpec(memory_space=VMEM)],
            out_specs=[pl.BlockSpec(memory_space=pl.ANY)] * 2,
            scratch_shapes=[
                pltpu.VMEM((2,) + lines, jnp.float32),
                pltpu.SemaphoreType.DMA((2,)),
            ],
            name="combine",
        )(in_vmem(blocks))
        return [value.reshape(shape) for value in results]
    tail = 3 * plan.own_layers * plan.rows
    scalars = coefficients(blocks[:, tail, :])
    fields = blocks[:, :tail].reshape(plan.devices, plan.own_layers, 3, plan.rows, plan.own)
    fields = fields.transpose(2, 1, 3, 0, 4).reshape((3,) + shape)
    near, far = weights_of([value[0, 0] for value in scalars])
    a, b, c = fields
    return near * a + far * b, a - (near * b + far * c)


def per_device(mesh, measured_slopes, valid_mask, layer_offsets, reg_weight):
    dirs, _, rows, width = measured_slopes.shape
    plan = Plan(mesh, dirs, rows, width, reg_weight.shape[0])
    column_tiles = width // LANES
    slopes = measured_slopes.reshape(dirs, 2, rows, column_tiles, LANES)
    slopes = slopes.transpose(0, 2, 3, 1, 4).reshape(dirs, rows, 2 * column_tiles, LANES)
    strips = plan.strip // LANES
    piece = (plan.tiles, plan.sent_tiles, plan.in_rows, LANES)
    if plan.direct:
        piece = (round_up(plan.sent_tiles * plan.used_rows, 8), LANES)
    kind = pltpu.VMEM if plan.direct else jax.ShapeDtypeStruct

    def gather(slots, after):
        return pl.pallas_call(
            functools.partial(gather_kernel, plan, slots),
            out_shape=[kind(piece, jnp.float32)] * len(slots),
            in_specs=[pl.BlockSpec(memory_space=pl.ANY)] * (2 + len(after)),
            out_specs=[pl.BlockSpec(memory_space=VMEM)] * len(slots),
            scratch_shapes=[
                pltpu.VMEM((dirs, plan.high, plan.raw_rows, LANES), jnp.float32),
                pltpu.VMEM((rows, plan.strip), jnp.int32),
                pltpu.VMEM((strips, plan.in_rows, LANES), jnp.float32),
                pltpu.VMEM((strips - 1, plan.in_rows, LANES), jnp.float32),
                pltpu.SemaphoreType.DMA((dirs + 1,)),
            ],
            cost_estimate=pl.CostEstimate(
                flops=10_000_000, bytes_accessed=2_000_000, transcendentals=0
            ),
            name="gather",
        )(slopes, valid_mask, *after)

    if plan.halves == 2:
        far = gather((2, 3), ())
        sent = gather((0, 1), far[:1]) + far
    else:
        sent = gather(tuple(range(plan.outs)), ())
    if plan.direct:
        fields = list(sent)
        for k in reversed(range(1, plan.outs)):
            fields[k] = lax.ppermute(sent[k], "tile", [(i, i ^ (2 * k)) for i in range(plan.tiles)])
        swap = [(i, i ^ 1) for i in range(plan.tiles)]
        fields = fields + [lax.ppermute(field, "tile", swap) for field in fields]
    else:
        fields = [lax.all_to_all(sent[0], "tile", 0, 0)]
    fields = [in_vmem(field) for field in fields]
    tall_rows = plan.grid_rows + 2 * PAD

    def scratch(*lead):
        return pltpu.VMEM(lead + (plan.lane_tiles, tall_rows, LANES), jnp.float32)

    blocks = pl.pallas_call(
        functools.partial(solve_kernel, plan),
        out_shape=kind((plan.devices, plan.out_rows, plan.own), jnp.float32),
        in_specs=[pl.BlockSpec(memory_space=SMEM)] * 2
        + [pl.BlockSpec(memory_space=VMEM)] * len(fields),
        out_specs=pl.BlockSpec(memory_space=VMEM),
        scratch_shapes=[
            scratch(dirs),
            scratch(),
            scratch(plan.layers),
            scratch(plan.layers),
            scratch(dirs, 2),
            scratch(plan.layers),
            pltpu.VMEM((3, plan.layers, plan.grid_rows, LANES), jnp.float32),
        ],
        name="solve",
    )(layer_offsets.transpose(1, 2, 0), reg_weight, *fields)
    blocks = lax.all_to_all(blocks, ("layer", "tile"), 0, 0)
    return tuple(combine(plan, blocks))


def solution(mesh):
    return jax.shard_map(
        functools.partial(per_device, mesh),
        mesh=mesh,
        in_specs=(P(None, None, "tile", None), P("tile", None), P(), P()),
        out_specs=(P("layer", "tile", None), P("layer", "tile", None)),
        check_vma=False,
    )
```

```python
import functools

import jax
import jax.numpy as jnp
from jax import lax
from jax.experimental import pallas as pl
from jax.experimental.pallas import tpu as pltpu
from jax.sharding import PartitionSpec as P

HALO = 8
LANES = 128
PAD = 8
REACH_ROW = 2 * (2 * HALO + 1)
REACH = REACH_ROW + HALO + 1
VMEM = pltpu.MemorySpace.VMEM
SMEM = pltpu.MemorySpace.SMEM


def round_up(value, unit):
    return -(-value // unit) * unit


class Plan:
    def __init__(self, mesh, dirs, rows, width, layers):
        self.layer_devices = mesh.shape["layer"]
        self.tiles = mesh.shape["tile"]
        self.devices = self.layer_devices * self.tiles
        self.dirs = dirs
        self.rows = rows
        self.width = width
        self.layers = layers
        self.own_layers = layers // self.layer_devices
        self.grid_rows = rows * self.tiles
        assert width % self.devices == 0 and layers % self.layer_devices == 0
        self.own = width // self.devices
        self.part = width // self.layer_devices
        assert self.part % LANES == 0
        self.lane_tiles = round_up(self.own + 2 * REACH, LANES) // LANES
        self.side = (self.lane_tiles * LANES - self.own) // 2
        self.margin = round_up(self.side + 1, LANES)
        self.high = round_up(rows + 1, 8)
        self.used_rows = dirs * (rows + 1) + rows
        self.in_rows = round_up(self.used_rows, 8)
        self.out_rows = round_up(3 * self.own_layers * rows + 1, 8)
        self.chips = self.tiles // 2
        self.direct = self.tiles in (2, 4, 8) and self.own == LANES and self.lane_tiles == 2
        self.outs = self.chips if self.direct else 1
        self.halves = 1
        if self.direct and self.chips == 4 and self.part % (8 * LANES) == 0:
            self.halves = 2
        self.stretch = self.part // self.halves
        self.strip = self.stretch + 2 * self.margin
        assert self.margin <= 4 * LANES and (2 * self.stretch // LANES) % 8 == 0
        self.raw_core = min(2 * self.stretch // LANES + 16, 2 * width // LANES)
        self.raw_rows = 2 * self.stretch // LANES + 32
        assert self.strip <= width
        self.sent_tiles = self.lane_tiles + 1 if self.direct else self.lane_tiles
        self.chunk = self.grid_rows
        while self.chunk > (96 if self.direct else 192):
            self.chunk //= 2


def in_vmem(value):
    return pltpu.with_memory_space_constraint(value, VMEM)


def lane_index():
    return lax.broadcasted_iota(jnp.int32, (8, LANES), 1)


def tall(mask, rows):
    return jnp.broadcast_to(mask[:1], (rows, LANES))


def lane_shift(tiles, steps, rows):
    count = len(tiles)
    if isinstance(steps, int):
        turn = (-steps) % LANES
    else:
        turn = jnp.where(steps > 0, LANES - steps, -steps)
    turned = [pltpu.roll(tile, turn, 1) for tile in tiles]
    if count == 1:
        return turned
    source = lane_index() + steps
    past = tall(source >= LANES, rows)
    before = tall(source < 0, rows)
    if count == 2:
        outside = past | before
        return [jnp.where(outside, turned[1 - t], turned[t]) for t in range(2)]
    return [
        jnp.where(
            past,
            turned[(t + 1) % count],
            jnp.where(before, turned[(t - 1) % count], turned[t]),
        )
        for t in range(count)
    ]


def place_of():
    return lax.axis_index("layer"), lax.axis_index("tile")


def gather_kernel(plan, slots, slopes, mask, *refs):
    count = len(slots) if plan.direct else 1
    outs, (raw, raw_mask, strip, ready, sems) = refs[-5 - count : -5], refs[-5:]
    layer, tile = place_of()
    rows, dirs, width = plan.rows, plan.dirs, plan.width
    side = plan.margin
    stretch = layer * plan.halves
    if plan.halves == 2:
        stretch = stretch + (((tile // 2) ^ slots[0]) // 2)
    column = stretch * plan.stretch - side
    line = stretch * (2 * plan.stretch // LANES)
    base = jnp.clip(column, 0, width - plan.strip)
    base_line = jnp.clip(line - 8, 0, 2 * width // LANES - plan.raw_core)
    slope_copies = [
        pltpu.make_async_copy(
            slopes.at[g, :, pl.ds(pl.multiple_of(base_line, 8), plan.raw_core), :],
            raw.at[g, pl.ds(0, rows), pl.ds(8, plan.raw_core), :],
            sems.at[g],
        )
        for g in range(dirs)
    ]
    mask_copy = pltpu.make_async_copy(
        mask.at[:, pl.ds(pl.multiple_of(base, LANES), plan.strip)], raw_mask, sems.at[dirs]
    )
    mask_copy.start()
    for copy in slope_copies:
        copy.start()
    mask_copy.wait()

    strips = plan.strip // LANES
    high = plan.high
    used = dirs * (rows + 1) + rows
    lane = lane_index()
    wrap = tall(lane == 0, high)
    blank = jnp.zeros((high - rows, LANES), jnp.float32)
    valid = []
    for n in range(strips):
        at = jnp.clip(column + n * LANES - base, 0, plan.strip - LANES)
        here = raw_mask[:, pl.ds(pl.multiple_of(at, LANES), LANES)].astype(jnp.float32)
        begin = column + n * LANES
        keep = jnp.where((begin >= 0) & (begin < width), here, 0.0)
        strip[n, dirs * rows : (dirs + 1) * rows, :] = keep
        if used < plan.in_rows:
            strip[n, used:, :] = jnp.zeros((plan.in_rows - used, LANES), jnp.float32)
        valid.append(keep > 0.0)
    for g in range(dirs):
        slope_copies[g].wait()
        flat = raw.at[g].reshape(high * plan.raw_rows, LANES)
        before = None
        for n in range(strips):
            at = line - base_line + 2 * n + 8 - 2 * (side // LANES)
            slope_x = flat[pl.ds(at, rows, stride=plan.raw_rows), :]
            slope_y = flat[pl.ds(at + 1, rows, stride=plan.raw_rows), :]
            both = jnp.concatenate([jnp.where(valid[n], slope_x + slope_y, 0.0), blank], axis=0)
            diff = jnp.concatenate([jnp.where(valid[n], slope_x - slope_y, 0.0), blank], axis=0)
            c = pltpu.roll(diff + pltpu.roll(both, 1, 0), 1, 1)
            shifted = c if before is None else jnp.where(wrap, before, c)
            before = c
            field = shifted - (both + pltpu.roll(diff, 1, 0))
            if n >= strips - side // LANES:
                inside = column + n * LANES + lane < width
                field = jnp.where(tall(inside, high), field, 0.0)
            strip[n, g * rows : (g + 1) * rows, :] = field[:rows]
            carry = (dirs + 1) * rows + g
            strip[n, carry : carry + 1, :] = field[rows : rows + 1]
    turned = {}

    def turn(n, by):
        if by == 0:
            return strip[n]
        for at in (n, n + 1):
            if (at, by) not in turned:
                turned[at, by] = pltpu.roll(strip[at], (-by) % LANES, 1)
        near = tall(lane < LANES - by, plan.in_rows)
        return jnp.where(near, turned[n, by], turned[n + 1, by])

    begin = plan.margin - plan.side
    if plan.direct:
        near = plan.chips // plan.halves
        for n in range(2 * near + 1):
            ready[n] = turn(begin // LANES + n, begin % LANES)
        for k, out in zip(slots, outs):
            at = 2 * (((tile // 2) ^ k) % near)
            for n in range(plan.sent_tiles):
                out[plan.used_rows * n : plan.used_rows * (n + 1), :] = ready[
                    at + n, : plan.used_rows, :
                ]
        return
    for t in range(plan.tiles):
        at = begin + t * plan.own
        for n in range(plan.lane_tiles):
            outs[0][t, n] = turn(at // LANES + n, at % LANES)


def solve_kernel(plan, all_offsets, all_weights, *refs):
    count = 2 * plan.outs if plan.direct else 1
    fields, (out, q, keep, v0, v1, phase, smooth, packed, offsets, weights, sems) = (
        refs[:count],
        refs[count:],
    )
    scalars_in = [
        pltpu.make_async_copy(all_offsets, offsets, sems.at[0]),
        pltpu.make_async_copy(all_weights, weights, sems.at[1]),
    ]
    for copy in scalars_in:
        copy.start()
    layers, dirs, rows = plan.layers, plan.dirs, plan.rows
    total, tiles = plan.grid_rows, range(plan.lane_tiles)
    chunk = plan.chunk
    starts = range(0, total, chunk)
    unrolled = plan.direct
    layer_place, tile_place = place_of()
    first = (layer_place * plan.tiles + tile_place) * plan.own - plan.side
    lane = lane_index()
    in_grid = []
    owned = []
    for t in tiles:
        local = lane + t * LANES
        column = local + first
        in_grid.append(tall(jnp.where((column >= 0) & (column < plan.width), 1.0, 0.0), chunk))
        owned.append(tall((local >= plan.side) & (local < plan.side + plan.own), chunk))
    two = plan.lane_tiles == 2 and plan.own == LANES

    def pack(window):
        if two:
            return jnp.where(owned[1], window[1], window[0])
        value = jnp.where(owned[0], window[0], 0.0)
        for t in tiles[1:]:
            value = jnp.where(owned[t], window[t], value)
        return value

    def packed_shift(window, steps):
        if not two:
            return pack(lane_shift(window, steps, chunk))
        turn = (-steps) % LANES if isinstance(steps, int) else jnp.where(steps > 0, LANES - steps, -steps)
        low = tall(lane < plan.side + steps, chunk)
        return pltpu.roll(jnp.where(low, window[1], window[0]), turn, 1)

    edge = jnp.zeros((PAD, LANES), jnp.float32)
    above, below = slice(0, PAD), slice(PAD + total, PAD + total + PAD)
    for t in tiles:
        keep[t, above, :] = edge
        keep[t, below, :] = edge
        for g in range(dirs):
            q[g, t, above, :] = edge
            q[g, t, below, :] = edge
            for i in range(2):
                phase[g, i, t, above, :] = edge
                phase[g, i, t, below, :] = edge
        for layer in range(layers):
            for ref in (v0, v1, smooth):
                ref[layer, t, above, :] = edge
                ref[layer, t, below, :] = edge
    sources = []
    if plan.direct:
        core = tile_place % 2
        for i, field in enumerate(fields):
            tile = 2 * ((tile_place // 2) ^ (i % plan.outs)) + (core if i < plan.outs else 1 - core)
            low = [(core + t) * plan.used_rows for t in tiles]
            sources.append((tile, [(field, start) for start in low]))
    else:
        for tile in range(plan.tiles):
            sources.append((tile, [(fields[0].at[tile, t], 0) for t in tiles]))
    for tile, windows in sources:
        here = pl.ds(PAD + tile * rows, rows)
        for t, (window, start) in enumerate(windows):
            keep[t, here, :] = window[pl.ds(start + dirs * rows, rows), :]
            for g in range(dirs):
                q[g, t, here, :] = window[pl.ds(start + g * rows, rows), :]
    for tile, windows in sources:
        below = pl.ds(PAD + (tile + 1) * rows, 1)
        counts = jnp.where(tile + 1 < plan.tiles, 1.0, 0.0)
        for t, (window, start) in enumerate(windows):
            for g in range(dirs):
                carry = start + (dirs + 1) * rows + g
                q[g, t, below, :] += window[pl.ds(carry, 1), :] * counts

    def four(x, up, down, left, right):
        return 4.0 * x - (up + down) - (left + right)

    def rows_at(r, by=0):
        return slice(PAD + r + by, PAD + r + by + chunk)

    def staged(first, second):
        for i, r in enumerate(starts):
            first(r)
            if i:
                second(starts[i - 1])
        second(starts[-1])

    def laplace(ref, layer, r, shift):
        x = [ref[layer, t, rows_at(r), :] for t in tiles]
        right = shift(x, 1)
        left = shift(x, -1)
        column = [
            4.0 * x[t] - (ref[layer, t, rows_at(r, -1), :] + ref[layer, t, rows_at(r, 1), :])
            for t in tiles
        ]
        if shift is packed_shift:
            return [pack(column) - (left + right)]
        return [column[t] - (left[t] + right[t]) for t in tiles]

    def window_shift(window, steps):
        return lane_shift(window, steps, chunk)

    def back_project(layer, level):
        source = (None, v0, v1)[level]
        shift = packed_shift if level == 2 else window_shift

        def smoothing(r):
            if source is not None:
                for t, value in enumerate(laplace(source, layer, r, window_shift)):
                    smooth[layer, t, rows_at(r), :] = value * in_grid[t]

        def adding(r):
            sums = None
            for g in range(dirs):
                low = PAD + r - offsets[layer, 0, g]
                window = [q[g, t, pl.ds(low, chunk), :] for t in tiles]
                moved = shift(window, -offsets[layer, 1, g])
                moved = [moved] if level == 2 else moved
                sums = moved if sums is None else [s + m for s, m in zip(sums, moved)]
            sums = [0.5 * value for value in sums]
            if source is not None:
                weight = weights[layer]
                sums = [s + weight * value for s, value in zip(sums, laplace(smooth, layer, r, shift))]
            if level == 2:
                packed[2, layer, r : r + chunk, :] = sums[0]
                return
            sums = [s * inside for s, inside in zip(sums, in_grid)]
            for t in tiles:
                (v0, v1)[level][layer, t, rows_at(r), :] = sums[t]
            packed[level, layer, r : r + chunk, :] = pack(sums)

        staged(smoothing, adding)

    def project(g, source):
        def phases(r):
            sums = None
            for layer in range(layers):
                low = PAD + r + offsets[layer, 0, g]
                window = [source[layer, t, pl.ds(low, chunk), :] for t in tiles]
                moved = lane_shift(window, offsets[layer, 1, g], chunk)
                sums = moved if sums is None else [s + m for s, m in zip(sums, moved)]
            sums = [s * inside for s, inside in zip(sums, in_grid)]
            right = lane_shift(sums, 1, chunk)
            for t in tiles:
                phase[g, 0, t, rows_at(r), :] = sums[t]
                phase[g, 1, t, rows_at(r), :] = right[t]

        def slopes(r):
            ahead, level = [], []
            for t in tiles:
                p00, p01 = phase[g, 0, t, rows_at(r), :], phase[g, 1, t, rows_at(r), :]
                p10, p11 = phase[g, 0, t, rows_at(r, 1), :], phase[g, 1, t, rows_at(r, 1), :]
                up0, up1 = phase[g, 0, t, rows_at(r, -1), :], phase[g, 1, t, rows_at(r, -1), :]
                mask, mask_up = keep[t, rows_at(r), :], keep[t, rows_at(r, -1), :]
                ahead.append(mask * (p01 - p10) + mask_up * (p01 - up0))
                level.append(mask * (p11 - p00) + mask_up * (up1 - p00))
            ahead = lane_shift(ahead, -1, chunk)
            for t in tiles:
                q[g, t, rows_at(r), :] = (ahead[t] - level[t]) * in_grid[t]

        staged(phases, slopes)

    def each(count, body):
        if unrolled:
            for i in range(count):
                body(i)
            return

        def step(i, carry):
            body(i)
            return carry

        lax.fori_loop(0, count, step, 0)

    def fold(value):
        return jnp.sum(value.reshape(chunk // 8, 8, LANES), axis=0)

    def inner(terms, layer, sums):
        for r in starts:
            values = terms([packed[i, layer, r : r + chunk, :] for i in range(3)])
            sums = [s + fold(value) for s, value in zip(sums, values)]
        return sums

    def send(i, layer):
        device, own = layer // plan.own_layers, layer % plan.own_layers
        for s in range(plan.tiles):
            block = packed[i, layer, s * rows : (s + 1) * rows, :]
            if plan.own < LANES:
                block = pltpu.roll(block, (-plan.side) % LANES, 1)[:, : plan.own]
            at = (own * 3 + i) * rows
            out[device * plan.tiles + s, at : at + rows, :] = block

    def first_terms(fields):
        a, b, _ = fields
        return a * a, a * b, b * b

    for copy in scalars_in:
        copy.wait()
    each(layers, lambda layer: back_project(layer, 0))
    each(dirs, lambda g: project(g, v0))
    each(layers, lambda layer: back_project(layer, 1))
    def second_terms(fields):
        a, b, c = fields
        e = a - spread * b
        f = b - spread * c
        return e * e, e * b, e * f, e * c + b * f, b * c

    sums = [jnp.zeros((8, LANES), jnp.float32)] * 3
    more = [jnp.zeros((8, LANES), jnp.float32)] * 5
    if not unrolled:
        each(dirs, lambda g: project(g, v1))
    for i in range(max(layers, dirs)):
        if unrolled and i < dirs:
            project(i, v1)
        if i < layers:
            sums = inner(first_terms, i, sums)
            send(0, i)
            send(1, i)
    s00, s01, s11 = [jnp.sum(value, keepdims=True) for value in sums]
    coefficient = jnp.where(s11 > 0.0, s01 / jnp.where(s11 > 0.0, s11, 1.0), 0.0)
    spread = jnp.broadcast_to(coefficient, (chunk, LANES))
    if not unrolled:
        each(layers, lambda layer: back_project(layer, 2))
    for layer in range(layers):
        if unrolled:
            back_project(layer, 2)
        more = inner(second_terms, layer, more)
        send(2, layer)
    more = [jnp.sum(value, keepdims=True) for value in more]
    scalars = [s00, s01, s11, coefficient] + more
    row = jnp.zeros((1, LANES), jnp.float32)
    for i, value in enumerate(scalars):
        row = jnp.where(lane[:1] == i, value, row)
    tail = 3 * plan.own_layers * rows
    note = jnp.broadcast_to(row[:, : plan.own], (plan.out_rows - tail, plan.own))
    for to in range(plan.devices):
        out[to, tail:, :] = note


def coefficients(notes):
    s00, s01, s11, c, ee, eb, ef, mixed, bc = [notes[:, i : i + 1] for i in range(9)]

    def total(value):
        return jnp.sum(value, axis=0, keepdims=True)

    norm_0 = total(s00)
    power_0 = total(s01)
    alpha_0 = norm_0 / power_0
    delta = alpha_0 - c
    norm_1 = total(ee - 2.0 * delta * eb + delta * delta * s11)
    beta = norm_1 / norm_0
    power_1 = (
        total(ef - delta * mixed + delta * delta * bc)
        + 2.0 * beta * total(eb - delta * s11)
        + beta * beta * power_0
    )
    return alpha_0, beta, norm_1 / power_1


def weights_of(scalars):
    alpha_0, beta, alpha_1 = scalars
    return alpha_0 + alpha_1 * (1.0 + beta), -alpha_1 * alpha_0


def combine_kernel(plan, blocks, estimate, residual, lines, sems):
    rows = plan.rows
    tail = 3 * plan.own_layers * rows
    near, far = [
        jnp.broadcast_to(value, (rows, LANES))
        for value in weights_of(coefficients(blocks[:, tail, :]))
    ]
    copies = [
        pltpu.make_async_copy(lines.at[i], ref, sems.at[i])
        for i, ref in enumerate((estimate, residual))
    ]
    for i, copy in enumerate(copies):
        for k in range(plan.devices):
            for own in range(plan.own_layers):
                field = [
                    blocks[k, (own * 3 + j) * rows : (own * 3 + j + 1) * rows, :]
                    for j in range(i, i + 2)
                ]
                value = near * field[0] + far * field[1]
                if i:
                    value = blocks[k, own * 3 * rows : (own * 3 + 1) * rows, :] - value
                where = pl.ds(own * rows * plan.devices + k, rows, stride=plan.devices)
                lines.at[i][where, :] = pltpu.roll(value, (-plan.side) % LANES, 1)
        copy.start()
    for copy in copies:
        copy.wait()


def combine(plan, blocks):
    shape = (plan.own_layers, plan.rows, plan.width)
    if plan.own == LANES:
        lines = (plan.own_layers * plan.rows * plan.devices, LANES)
        results = pl.pallas_call(
            functools.partial(combine_kernel, plan),
            out_shape=[jax.ShapeDtypeStruct(lines, jnp.float32)] * 2,
            in_specs=[pl.BlockSpec(memory_space=VMEM)],
            out_specs=[pl.BlockSpec(memory_space=pl.ANY)] * 2,
            scratch_shapes=[
                pltpu.VMEM((2,) + lines, jnp.float32),
                pltpu.SemaphoreType.DMA((2,)),
            ],
            name="combine",
        )(in_vmem(blocks))
        return [value.reshape(shape) for value in results]
    tail = 3 * plan.own_layers * plan.rows
    scalars = coefficients(blocks[:, tail, :])
    fields = blocks[:, :tail].reshape(plan.devices, plan.own_layers, 3, plan.rows, plan.own)
    fields = fields.transpose(2, 1, 3, 0, 4).reshape((3,) + shape)
    near, far = weights_of([value[0, 0] for value in scalars])
    a, b, c = fields
    return near * a + far * b, a - (near * b + far * c)


def per_device(mesh, measured_slopes, valid_mask, layer_offsets, reg_weight):
    dirs, _, rows, width = measured_slopes.shape
    plan = Plan(mesh, dirs, rows, width, reg_weight.shape[0])
    column_tiles = width // LANES
    slopes = measured_slopes.reshape(dirs, 2, rows, column_tiles, LANES)
    slopes = slopes.transpose(0, 2, 3, 1, 4).reshape(dirs, rows, 2 * column_tiles, LANES)
    strips = plan.strip // LANES
    piece = (plan.tiles, plan.sent_tiles, plan.in_rows, LANES)
    if plan.direct:
        piece = (round_up(plan.sent_tiles * plan.used_rows, 8), LANES)
    kind = pltpu.VMEM if plan.direct else jax.ShapeDtypeStruct

    def gather(slots, after):
        return pl.pallas_call(
            functools.partial(gather_kernel, plan, slots),
            out_shape=[kind(piece, jnp.float32)] * len(slots),
            in_specs=[pl.BlockSpec(memory_space=pl.ANY)] * (2 + len(after)),
            out_specs=[pl.BlockSpec(memory_space=VMEM)] * len(slots),
            scratch_shapes=[
                pltpu.VMEM((dirs, plan.high, plan.raw_rows, LANES), jnp.float32),
                pltpu.VMEM((rows, plan.strip), jnp.int32),
                pltpu.VMEM((strips, plan.in_rows, LANES), jnp.float32),
                pltpu.VMEM((strips - 1, plan.in_rows, LANES), jnp.float32),
                pltpu.SemaphoreType.DMA((dirs + 1,)),
            ],
            cost_estimate=pl.CostEstimate(
                flops=10_000_000, bytes_accessed=2_000_000, transcendentals=0
            ),
            name="gather",
        )(slopes, valid_mask, *after)

    if plan.halves == 2:
        far = gather((2, 3), ())
        sent = gather((0, 1), far[:1]) + far
    else:
        sent = gather(tuple(range(plan.outs)), ())
    if plan.direct:
        fields = list(sent)
        for k in reversed(range(1, plan.outs)):
            fields[k] = lax.ppermute(sent[k], "tile", [(i, i ^ (2 * k)) for i in range(plan.tiles)])
        swap = [(i, i ^ 1) for i in range(plan.tiles)]
        fields = fields + [lax.ppermute(field, "tile", swap) for field in fields]
    else:
        fields = [lax.all_to_all(sent[0], "tile", 0, 0)]
    fields = [in_vmem(field) for field in fields]
    tall_rows = plan.grid_rows + 2 * PAD

    def scratch(*lead):
        return pltpu.VMEM(lead + (plan.lane_tiles, tall_rows, LANES), jnp.float32)

    blocks = pl.pallas_call(
        functools.partial(solve_kernel, plan),
        out_shape=kind((plan.devices, plan.out_rows, plan.own), jnp.float32),
        in_specs=[pl.BlockSpec(memory_space=pl.ANY)] * 2
        + [pl.BlockSpec(memory_space=VMEM)] * len(fields),
        out_specs=pl.BlockSpec(memory_space=VMEM),
        scratch_shapes=[
            scratch(dirs),
            scratch(),
            scratch(plan.layers),
            scratch(plan.layers),
            scratch(dirs, 2),
            scratch(plan.layers),
            pltpu.VMEM((3, plan.layers, plan.grid_rows, LANES), jnp.float32),
            pltpu.SMEM((plan.layers, 2, dirs), jnp.int32),
            pltpu.SMEM((plan.layers,), jnp.float32),
            pltpu.SemaphoreType.DMA((2,)),
        ],
        name="solve",
    )(layer_offsets.transpose(1, 2, 0), reg_weight, *fields)
    blocks = lax.all_to_all(blocks, ("layer", "tile"), 0, 0)
    return tuple(combine(plan, blocks))


def solution(mesh):
    return jax.shard_map(
        functools.partial(per_device, mesh),
        mesh=mesh,
        in_specs=(P(None, None, "tile", None), P("tile", None), P(), P()),
        out_specs=(P("layer", "tile", None), P("layer", "tile", None)),
        check_vma=False,
    )
```

```python
import functools

import jax
import jax.numpy as jnp
from jax import lax
from jax.experimental import pallas as pl
from jax.experimental.pallas import tpu as pltpu
from jax.sharding import PartitionSpec as P

HALO = 8
LANES = 128
PAD = 8
REACH_ROW = 2 * (2 * HALO + 1)
REACH = REACH_ROW + HALO + 1
VMEM = pltpu.MemorySpace.VMEM
SMEM = pltpu.MemorySpace.SMEM


def round_up(value, unit):
    return -(-value // unit) * unit


class Plan:
    def __init__(self, mesh, dirs, rows, width, layers):
        self.layer_devices = mesh.shape["layer"]
        self.tiles = mesh.shape["tile"]
        self.devices = self.layer_devices * self.tiles
        self.dirs = dirs
        self.rows = rows
        self.width = width
        self.layers = layers
        self.own_layers = layers // self.layer_devices
        self.grid_rows = rows * self.tiles
        assert width % self.devices == 0 and layers % self.layer_devices == 0
        self.own = width // self.devices
        self.part = width // self.layer_devices
        assert self.part % LANES == 0
        self.lane_tiles = round_up(self.own + 2 * REACH, LANES) // LANES
        self.side = (self.lane_tiles * LANES - self.own) // 2
        self.margin = round_up(self.side + 1, LANES)
        self.high = round_up(rows + 1, 8)
        self.used_rows = dirs * (rows + 1) + rows
        self.in_rows = round_up(self.used_rows, 8)
        self.out_rows = round_up(3 * self.own_layers * rows + 1, 8)
        self.chips = self.tiles // 2
        self.direct = self.tiles in (2, 4, 8) and self.own == LANES and self.lane_tiles == 2
        self.outs = self.chips if self.direct else 1
        self.halves = 1
        if self.direct and self.chips == 4 and self.part % (8 * LANES) == 0:
            self.halves = 2
        self.stretch = self.part // self.halves
        self.strip = self.stretch + 2 * self.margin
        assert self.margin <= 4 * LANES and (2 * self.stretch // LANES) % 8 == 0
        self.raw_core = min(2 * self.stretch // LANES + 16, 2 * width // LANES)
        self.raw_rows = 2 * self.stretch // LANES + 32
        assert self.strip <= width
        self.sent_tiles = self.lane_tiles + 1 if self.direct else self.lane_tiles
        self.chunk = self.grid_rows
        while self.chunk > (96 if self.direct else 192):
            self.chunk //= 2


def in_vmem(value):
    return pltpu.with_memory_space_constraint(value, VMEM)


def lane_index():
    return lax.broadcasted_iota(jnp.int32, (8, LANES), 1)


def tall(mask, rows):
    return jnp.broadcast_to(mask[:1], (rows, LANES))


def lane_shift(tiles, steps, rows):
    count = len(tiles)
    if isinstance(steps, int):
        turn = (-steps) % LANES
    else:
        turn = jnp.where(steps > 0, LANES - steps, -steps)
    if count == 2:
        lane = lane_index()
        other = tall((lane < steps) | (lane >= LANES + steps), rows)
        return [
            pltpu.roll(jnp.where(other, tiles[1 - t], tiles[t]), turn, 1) for t in range(2)
        ]
    turned = [pltpu.roll(tile, turn, 1) for tile in tiles]
    if count == 1:
        return turned
    source = lane_index() + steps
    past = tall(source >= LANES, rows)
    before = tall(source < 0, rows)
    return [
        jnp.where(
            past,
            turned[(t + 1) % count],
            jnp.where(before, turned[(t - 1) % count], turned[t]),
        )
        for t in range(count)
    ]


def place_of():
    return lax.axis_index("layer"), lax.axis_index("tile")


def gather_kernel(plan, slots, slopes, mask, *refs):
    count = len(slots) if plan.direct else 1
    outs, (raw, raw_mask, strip, ready, sems) = refs[-5 - count : -5], refs[-5:]
    layer, tile = place_of()
    rows, dirs, width = plan.rows, plan.dirs, plan.width
    side = plan.margin
    stretch = layer * plan.halves
    if plan.halves == 2:
        stretch = stretch + (((tile // 2) ^ slots[0]) // 2)
    column = stretch * plan.stretch - side
    line = stretch * (2 * plan.stretch // LANES)
    base = jnp.clip(column, 0, width - plan.strip)
    base_line = jnp.clip(line - 8, 0, 2 * width // LANES - plan.raw_core)
    slope_copies = [
        pltpu.make_async_copy(
            slopes.at[g, :, pl.ds(pl.multiple_of(base_line, 8), plan.raw_core), :],
            raw.at[g, pl.ds(0, rows), pl.ds(8, plan.raw_core), :],
            sems.at[g],
        )
        for g in range(dirs)
    ]
    mask_copy = pltpu.make_async_copy(
        mask.at[:, pl.ds(pl.multiple_of(base, LANES), plan.strip)], raw_mask, sems.at[dirs]
    )
    mask_copy.start()
    for copy in slope_copies:
        copy.start()
    mask_copy.wait()

    strips = plan.strip // LANES
    high = plan.high
    used = dirs * (rows + 1) + rows
    lane = lane_index()
    wrap = tall(lane == 0, high)
    blank = jnp.zeros((high - rows, LANES), jnp.float32)
    valid = []
    for n in range(strips):
        at = jnp.clip(column + n * LANES - base, 0, plan.strip - LANES)
        here = raw_mask[:, pl.ds(pl.multiple_of(at, LANES), LANES)].astype(jnp.float32)
        begin = column + n * LANES
        keep = jnp.where((begin >= 0) & (begin < width), here, 0.0)
        strip[n, dirs * rows : (dirs + 1) * rows, :] = keep
        if used < plan.in_rows:
            strip[n, used:, :] = jnp.zeros((plan.in_rows - used, LANES), jnp.float32)
        valid.append(keep > 0.0)
    for g in range(dirs):
        slope_copies[g].wait()
        flat = raw.at[g].reshape(high * plan.raw_rows, LANES)
        before = None
        for n in range(strips):
            at = line - base_line + 2 * n + 8 - 2 * (side // LANES)
            slope_x = flat[pl.ds(at, rows, stride=plan.raw_rows), :]
            slope_y = flat[pl.ds(at + 1, rows, stride=plan.raw_rows), :]
            both = jnp.concatenate([jnp.where(valid[n], slope_x + slope_y, 0.0), blank], axis=0)
            diff = jnp.concatenate([jnp.where(valid[n], slope_x - slope_y, 0.0), blank], axis=0)
            c = pltpu.roll(diff + pltpu.roll(both, 1, 0), 1, 1)
            shifted = c if before is None else jnp.where(wrap, before, c)
            before = c
            field = shifted - (both + pltpu.roll(diff, 1, 0))
            if n >= strips - side // LANES:
                inside = column + n * LANES + lane < width
                field = jnp.where(tall(inside, high), field, 0.0)
            strip[n, g * rows : (g + 1) * rows, :] = field[:rows]
            carry = (dirs + 1) * rows + g
            strip[n, carry : carry + 1, :] = field[rows : rows + 1]
    turned = {}

    def turn(n, by):
        if by == 0:
            return strip[n]
        for at in (n, n + 1):
            if (at, by) not in turned:
                turned[at, by] = pltpu.roll(strip[at], (-by) % LANES, 1)
        near = tall(lane < LANES - by, plan.in_rows)
        return jnp.where(near, turned[n, by], turned[n + 1, by])

    begin = plan.margin - plan.side
    if plan.direct:
        near = plan.chips // plan.halves
        for n in range(2 * near + 1):
            ready[n] = turn(begin // LANES + n, begin % LANES)
        for k, out in zip(slots, outs):
            at = 2 * (((tile // 2) ^ k) % near)
            for n in range(plan.sent_tiles):
                out[plan.used_rows * n : plan.used_rows * (n + 1), :] = ready[
                    at + n, : plan.used_rows, :
                ]
        return
    for t in range(plan.tiles):
        at = begin + t * plan.own
        for n in range(plan.lane_tiles):
            outs[0][t, n] = turn(at // LANES + n, at % LANES)


def solve_kernel(plan, all_offsets, all_weights, *refs):
    count = 2 * plan.outs if plan.direct else 1
    fields, (out, q, keep, v0, v1, phase, smooth, packed, offsets, weights, sems) = (
        refs[:count],
        refs[count:],
    )
    scalars_in = [
        pltpu.make_async_copy(all_offsets, offsets, sems.at[0]),
        pltpu.make_async_copy(all_weights, weights, sems.at[1]),
    ]
    for copy in scalars_in:
        copy.start()
    layers, dirs, rows = plan.layers, plan.dirs, plan.rows
    total, tiles = plan.grid_rows, range(plan.lane_tiles)
    chunk = plan.chunk
    starts = range(0, total, chunk)
    unrolled = plan.direct
    layer_place, tile_place = place_of()
    first = (layer_place * plan.tiles + tile_place) * plan.own - plan.side
    lane = lane_index()
    in_grid = []
    owned = []
    for t in tiles:
        local = lane + t * LANES
        column = local + first
        in_grid.append(tall(jnp.where((column >= 0) & (column < plan.width), 1.0, 0.0), chunk))
        owned.append(tall((local >= plan.side) & (local < plan.side + plan.own), chunk))
    two = plan.lane_tiles == 2 and plan.own == LANES

    def pack(window):
        if two:
            return jnp.where(owned[1], window[1], window[0])
        value = jnp.where(owned[0], window[0], 0.0)
        for t in tiles[1:]:
            value = jnp.where(owned[t], window[t], value)
        return value

    def packed_shift(window, steps):
        if not two:
            return pack(lane_shift(window, steps, chunk))
        turn = (-steps) % LANES if isinstance(steps, int) else jnp.where(steps > 0, LANES - steps, -steps)
        low = tall(lane < plan.side + steps, chunk)
        return pltpu.roll(jnp.where(low, window[1], window[0]), turn, 1)

    edge = jnp.zeros((PAD, LANES), jnp.float32)
    above, below = slice(0, PAD), slice(PAD + total, PAD + total + PAD)
    for t in tiles:
        keep[t, above, :] = edge
        keep[t, below, :] = edge
        for g in range(dirs):
            q[g, t, above, :] = edge
            q[g, t, below, :] = edge
            for i in range(2):
                phase[g, i, t, above, :] = edge
                phase[g, i, t, below, :] = edge
        for layer in range(layers):
            for ref in (v0, v1, smooth):
                ref[layer, t, above, :] = edge
                ref[layer, t, below, :] = edge
    sources = []
    if plan.direct:
        core = tile_place % 2
        for i, field in enumerate(fields):
            tile = 2 * ((tile_place // 2) ^ (i % plan.outs)) + (core if i < plan.outs else 1 - core)
            low = [(core + t) * plan.used_rows for t in tiles]
            sources.append((tile, [(field, start) for start in low]))
    else:
        for tile in range(plan.tiles):
            sources.append((tile, [(fields[0].at[tile, t], 0) for t in tiles]))
    for tile, windows in sources:
        here = pl.ds(PAD + tile * rows, rows)
        for t, (window, start) in enumerate(windows):
            keep[t, here, :] = window[pl.ds(start + dirs * rows, rows), :]
            for g in range(dirs):
                q[g, t, here, :] = window[pl.ds(start + g * rows, rows), :]
    for tile, windows in sources:
        below = pl.ds(PAD + (tile + 1) * rows, 1)
        counts = jnp.where(tile + 1 < plan.tiles, 1.0, 0.0)
        for t, (window, start) in enumerate(windows):
            for g in range(dirs):
                carry = start + (dirs + 1) * rows + g
                q[g, t, below, :] += window[pl.ds(carry, 1), :] * counts

    def four(x, up, down, left, right):
        return 4.0 * x - (up + down) - (left + right)

    def rows_at(r, by=0):
        return slice(PAD + r + by, PAD + r + by + chunk)

    def staged(first, second):
        for i, r in enumerate(starts):
            first(r)
            if i:
                second(starts[i - 1])
        second(starts[-1])

    def laplace(ref, layer, r, shift):
        x = [ref[layer, t, rows_at(r), :] for t in tiles]
        right = shift(x, 1)
        left = shift(x, -1)
        column = [
            4.0 * x[t] - (ref[layer, t, rows_at(r, -1), :] + ref[layer, t, rows_at(r, 1), :])
            for t in tiles
        ]
        if shift is packed_shift:
            return [pack(column) - (left + right)]
        return [column[t] - (left[t] + right[t]) for t in tiles]

    def window_shift(window, steps):
        return lane_shift(window, steps, chunk)

    def back_project(layer, level):
        source = (None, v0, v1)[level]
        shift = packed_shift if level == 2 else window_shift

        def smoothing(r):
            if source is not None:
                for t, value in enumerate(laplace(source, layer, r, window_shift)):
                    smooth[layer, t, rows_at(r), :] = value * in_grid[t]

        def adding(r):
            sums = None
            for g in range(dirs):
                low = PAD + r - offsets[layer, 0, g]
                window = [q[g, t, pl.ds(low, chunk), :] for t in tiles]
                moved = shift(window, -offsets[layer, 1, g])
                moved = [moved] if level == 2 else moved
                sums = moved if sums is None else [s + m for s, m in zip(sums, moved)]
            if level:
                sums = [0.5 * value for value in sums]
            if source is not None:
                weight = weights[layer]
                sums = [s + weight * value for s, value in zip(sums, laplace(smooth, layer, r, shift))]
            if level == 2:
                packed[2, layer, r : r + chunk, :] = sums[0]
                return
            scale = in_grid if level else [0.5 * inside for inside in in_grid]
            sums = [s * inside for s, inside in zip(sums, scale)]
            for t in tiles:
                (v0, v1)[level][layer, t, rows_at(r), :] = sums[t]
            packed[level, layer, r : r + chunk, :] = pack(sums)

        staged(smoothing, adding)

    def project(g, source):
        def phases(r):
            sums = None
            for layer in range(layers):
                low = PAD + r + offsets[layer, 0, g]
                window = [source[layer, t, pl.ds(low, chunk), :] for t in tiles]
                moved = lane_shift(window, offsets[layer, 1, g], chunk)
                sums = moved if sums is None else [s + m for s, m in zip(sums, moved)]
            sums = [s * inside for s, inside in zip(sums, in_grid)]
            right = lane_shift(sums, 1, chunk)
            for t in tiles:
                phase[g, 0, t, rows_at(r), :] = sums[t]
                phase[g, 1, t, rows_at(r), :] = right[t]

        def slopes(r):
            ahead, level = [], []
            for t in tiles:
                p00, p01 = phase[g, 0, t, rows_at(r), :], phase[g, 1, t, rows_at(r), :]
                p10, p11 = phase[g, 0, t, rows_at(r, 1), :], phase[g, 1, t, rows_at(r, 1), :]
                up0, up1 = phase[g, 0, t, rows_at(r, -1), :], phase[g, 1, t, rows_at(r, -1), :]
                mask, mask_up = keep[t, rows_at(r), :], keep[t, rows_at(r, -1), :]
                ahead.append(mask * (p01 - p10) + mask_up * (p01 - up0))
                level.append(mask * (p11 - p00) + mask_up * (up1 - p00))
            ahead = lane_shift(ahead, -1, chunk)
            for t in tiles:
                q[g, t, rows_at(r), :] = (ahead[t] - level[t]) * in_grid[t]

        staged(phases, slopes)

    def each(count, body):
        if unrolled:
            for i in range(count):
                body(i)
            return

        def step(i, carry):
            body(i)
            return carry

        lax.fori_loop(0, count, step, 0)

    def fold(value):
        return jnp.sum(value.reshape(chunk // 8, 8, LANES), axis=0)

    def inner(terms, layer, sums):
        for r in starts:
            values = terms([packed[i, layer, r : r + chunk, :] for i in range(3)])
            sums = [s + fold(value) for s, value in zip(sums, values)]
        return sums

    def send(i, layer):
        device, own = layer // plan.own_layers, layer % plan.own_layers
        for s in range(plan.tiles):
            block = packed[i, layer, s * rows : (s + 1) * rows, :]
            if plan.own < LANES:
                block = pltpu.roll(block, (-plan.side) % LANES, 1)[:, : plan.own]
            at = (own * 3 + i) * rows
            out[device * plan.tiles + s, at : at + rows, :] = block

    def first_terms(fields):
        a, b, _ = fields
        return a * a, a * b, b * b

    for copy in scalars_in:
        copy.wait()
    each(layers, lambda layer: back_project(layer, 0))
    each(dirs, lambda g: project(g, v0))
    each(layers, lambda layer: back_project(layer, 1))
    def second_terms(fields):
        a, b, c = fields
        e = a - spread * b
        f = b - spread * c
        return e * e, e * b, e * f, e * c + b * f, b * c

    sums = [jnp.zeros((8, LANES), jnp.float32)] * 3
    more = [jnp.zeros((8, LANES), jnp.float32)] * 5
    if not unrolled:
        each(dirs, lambda g: project(g, v1))
    for i in range(max(layers, dirs)):
        if unrolled and i < dirs:
            project(i, v1)
        if i < layers:
            sums = inner(first_terms, i, sums)
            send(0, i)
            send(1, i)
    s00, s01, s11 = [jnp.sum(value, keepdims=True) for value in sums]
    coefficient = jnp.where(s11 > 0.0, s01 / jnp.where(s11 > 0.0, s11, 1.0), 0.0)
    spread = jnp.broadcast_to(coefficient, (chunk, LANES))
    if not unrolled:
        each(layers, lambda layer: back_project(layer, 2))
    for layer in range(layers):
        if unrolled:
            back_project(layer, 2)
        more = inner(second_terms, layer, more)
        send(2, layer)
    more = [jnp.sum(value, keepdims=True) for value in more]
    scalars = [s00, s01, s11, coefficient] + more
    row = jnp.zeros((1, LANES), jnp.float32)
    for i, value in enumerate(scalars):
        row = jnp.where(lane[:1] == i, value, row)
    tail = 3 * plan.own_layers * rows
    note = jnp.broadcast_to(row[:, : plan.own], (plan.out_rows - tail, plan.own))
    for to in range(plan.devices):
        out[to, tail:, :] = note


def coefficients(notes):
    s00, s01, s11, c, ee, eb, ef, mixed, bc = [notes[:, i : i + 1] for i in range(9)]

    def total(value):
        return jnp.sum(value, axis=0, keepdims=True)

    norm_0 = total(s00)
    power_0 = total(s01)
    alpha_0 = norm_0 / power_0
    delta = alpha_0 - c
    norm_1 = total(ee - 2.0 * delta * eb + delta * delta * s11)
    beta = norm_1 / norm_0
    power_1 = (
        total(ef - delta * mixed + delta * delta * bc)
        + 2.0 * beta * total(eb - delta * s11)
        + beta * beta * power_0
    )
    return alpha_0, beta, norm_1 / power_1


def weights_of(scalars):
    alpha_0, beta, alpha_1 = scalars
    return alpha_0 + alpha_1 * (1.0 + beta), -alpha_1 * alpha_0


def combine_kernel(plan, blocks, estimate, residual, lines, sems):
    rows = plan.rows
    tail = 3 * plan.own_layers * rows
    near, far = [
        jnp.broadcast_to(value, (rows, LANES))
        for value in weights_of(coefficients(blocks[:, tail, :]))
    ]
    copies = [
        pltpu.make_async_copy(lines.at[i], ref, sems.at[i])
        for i, ref in enumerate((estimate, residual))
    ]
    for i, copy in enumerate(copies):
        for k in range(plan.devices):
            for own in range(plan.own_layers):
                field = [
                    blocks[k, (own * 3 + j) * rows : (own * 3 + j + 1) * rows, :]
                    for j in range(i, i + 2)
                ]
                value = near * field[0] + far * field[1]
                if i:
                    value = blocks[k, own * 3 * rows : (own * 3 + 1) * rows, :] - value
                where = pl.ds(own * rows * plan.devices + k, rows, stride=plan.devices)
                lines.at[i][where, :] = pltpu.roll(value, (-plan.side) % LANES, 1)
        copy.start()
    for copy in copies:
        copy.wait()


def combine(plan, blocks):
    shape = (plan.own_layers, plan.rows, plan.width)
    if plan.own == LANES:
        lines = (plan.own_layers * plan.rows * plan.devices, LANES)
        results = pl.pallas_call(
            functools.partial(combine_kernel, plan),
            out_shape=[jax.ShapeDtypeStruct(lines, jnp.float32)] * 2,
            in_specs=[pl.BlockSpec(memory_space=VMEM)],
            out_specs=[pl.BlockSpec(memory_space=pl.ANY)] * 2,
            scratch_shapes=[
                pltpu.VMEM((2,) + lines, jnp.float32),
                pltpu.SemaphoreType.DMA((2,)),
            ],
            name="combine",
        )(in_vmem(blocks))
        return [value.reshape(shape) for value in results]
    tail = 3 * plan.own_layers * plan.rows
    scalars = coefficients(blocks[:, tail, :])
    fields = blocks[:, :tail].reshape(plan.devices, plan.own_layers, 3, plan.rows, plan.own)
    fields = fields.transpose(2, 1, 3, 0, 4).reshape((3,) + shape)
    near, far = weights_of([value[0, 0] for value in scalars])
    a, b, c = fields
    return near * a + far * b, a - (near * b + far * c)


def per_device(mesh, measured_slopes, valid_mask, layer_offsets, reg_weight):
    dirs, _, rows, width = measured_slopes.shape
    plan = Plan(mesh, dirs, rows, width, reg_weight.shape[0])
    column_tiles = width // LANES
    slopes = measured_slopes.reshape(dirs, 2, rows, column_tiles, LANES)
    slopes = slopes.transpose(0, 2, 3, 1, 4).reshape(dirs, rows, 2 * column_tiles, LANES)
    strips = plan.strip // LANES
    piece = (plan.tiles, plan.sent_tiles, plan.in_rows, LANES)
    if plan.direct:
        piece = (round_up(plan.sent_tiles * plan.used_rows, 8), LANES)
    kind = pltpu.VMEM if plan.direct else jax.ShapeDtypeStruct

    def gather(slots, after):
        return pl.pallas_call(
            functools.partial(gather_kernel, plan, slots),
            out_shape=[kind(piece, jnp.float32)] * len(slots),
            in_specs=[pl.BlockSpec(memory_space=pl.ANY)] * (2 + len(after)),
            out_specs=[pl.BlockSpec(memory_space=VMEM)] * len(slots),
            scratch_shapes=[
                pltpu.VMEM((dirs, plan.high, plan.raw_rows, LANES), jnp.float32),
                pltpu.VMEM((rows, plan.strip), jnp.int32),
                pltpu.VMEM((strips, plan.in_rows, LANES), jnp.float32),
                pltpu.VMEM((strips - 1, plan.in_rows, LANES), jnp.float32),
                pltpu.SemaphoreType.DMA((dirs + 1,)),
            ],
            cost_estimate=pl.CostEstimate(
                flops=10_000_000, bytes_accessed=2_000_000, transcendentals=0
            ),
            name="gather",
        )(slopes, valid_mask, *after)

    if plan.halves == 2:
        far = gather((2, 3), ())
        sent = gather((0, 1), far[:1]) + far
    else:
        sent = gather(tuple(range(plan.outs)), ())
    if plan.direct:
        fields = list(sent)
        for k in reversed(range(1, plan.outs)):
            fields[k] = lax.ppermute(sent[k], "tile", [(i, i ^ (2 * k)) for i in range(plan.tiles)])
        swap = [(i, i ^ 1) for i in range(plan.tiles)]
        fields = fields + [lax.ppermute(field, "tile", swap) for field in fields]
    else:
        fields = [lax.all_to_all(sent[0], "tile", 0, 0)]
    fields = [in_vmem(field) for field in fields]
    tall_rows = plan.grid_rows + 2 * PAD

    def scratch(*lead):
        return pltpu.VMEM(lead + (plan.lane_tiles, tall_rows, LANES), jnp.float32)

    blocks = pl.pallas_call(
        functools.partial(solve_kernel, plan),
        out_shape=kind((plan.devices, plan.out_rows, plan.own), jnp.float32),
        in_specs=[pl.BlockSpec(memory_space=pl.ANY)] * 2
        + [pl.BlockSpec(memory_space=VMEM)] * len(fields),
        out_specs=pl.BlockSpec(memory_space=VMEM),
        scratch_shapes=[
            scratch(dirs),
            scratch(),
            scratch(plan.layers),
            scratch(plan.layers),
            scratch(dirs, 2),
            scratch(plan.layers),
            pltpu.VMEM((3, plan.layers, plan.grid_rows, LANES), jnp.float32),
            pltpu.SMEM((plan.layers, 2, dirs), jnp.int32),
            pltpu.SMEM((plan.layers,), jnp.float32),
            pltpu.SemaphoreType.DMA((2,)),
        ],
        name="solve",
    )(layer_offsets.transpose(1, 2, 0), reg_weight, *fields)
    blocks = lax.all_to_all(blocks, ("layer", "tile"), 0, 0)
    return tuple(combine(plan, blocks))


def solution(mesh):
    return jax.shard_map(
        functools.partial(per_device, mesh),
        mesh=mesh,
        in_specs=(P(None, None, "tile", None), P("tile", None), P(), P()),
        out_specs=(P("layer", "tile", None), P("layer", "tile", None)),
        check_vma=False,
    )
```
